32 devices in a mesh: tm: 4 (over x, core), rows: 8 (over z, y).
Axes of the slice: x: 2, y: 2, z: 4, core: 2. Of those that a mesh axis runs over, the one named last changes fastest.
Arguments:
- smoother_gains: bfloat16 [4, 1536, 1536], P('tm', 'rows'), may hold values from -1 to 1
- smoother_offsets: bfloat16 [4, 1536], P('tm', 'rows'), may hold values from -6 to 6
- smoother_covs: bfloat16 [4, 1536, 1536], P('tm', 'rows'), may hold values from -1 to 4, as said below
Outputs:
- smoothed_means: bfloat16 [4, 1536], P('tm', 'rows')
- smoothed_covs: bfloat16 [4, 1536, 1536], P('tm', 'rows')
The draws below stay inside these ranges and needn't reach their ends.
Inputs may be any that keep to these rules, and one draw needn't show every extreme that they name: `smoother_covs`: each step's covariance matrix is symmetric.
All inputs are finite; a program needn't handle non-finite values.
Results may differ from the reference program's by a relative error of at most 0.025.
Values may be sent and summed in bfloat16 or wider, within the bound.
A program may use at most 64 MiB of HBM per device.

```python
import math
import jax
import jax.numpy as jnp
from jax import lax

NS = 1536
STEPS = 4


def draw_smoother_gains(key, part):
    first_key, second_key = jax.random.split(jax.random.fold_in(key, 11))
    rate_diag = jax.random.uniform(first_key, (STEPS, NS), jnp.float32, 0.3, 0.95)
    noise_part = jax.random.normal(second_key, (STEPS, NS, NS), jnp.float32) * (0.3 / math.sqrt(NS))
    identity_mat = jnp.eye(NS, dtype=jnp.float32)
    combined = noise_part + identity_mat[None, :, :] * rate_diag[:, :, None]
    return jnp.clip(combined, -1.0, 1.0).astype(jnp.bfloat16)


def draw_smoother_covs(key, part):
    first_key, second_key = jax.random.split(jax.random.fold_in(key, 23))
    scale_diag = jnp.exp(jax.random.uniform(first_key, (STEPS, NS), jnp.float32, math.log(0.5), math.log(2.0)))
    noise_part = jax.random.normal(second_key, (STEPS, NS, NS), jnp.float32) * (0.1 / math.sqrt(NS))
    noise_part = jnp.clip(noise_part, -0.5, 0.5)
    symmetric = noise_part + jnp.swapaxes(noise_part, 1, 2)
    identity_mat = jnp.eye(NS, dtype=jnp.float32)
    return (symmetric + identity_mat[None, :, :] * scale_diag[:, :, None]).astype(jnp.bfloat16)


def block_levels(rng, dims, shards, low, high):
    level = 1.0
    for position, shards_of in shards:
        heights = jax.random.uniform(jax.random.fold_in(jax.random.fold_in(rng, 6), position), (shards_of,), jnp.float32, low / len(shards), high / len(shards))
        level = level * jnp.repeat(jnp.exp(heights), dims[position] // shards_of).reshape((-1,) + (1,) * (len(dims) - 1 - position))
    return level


def noise(own_key, dims, width, most, cuts=(), held_as=jnp.bfloat16):
    array = jax.random.normal(own_key, dims, jnp.float32) * width
    if len(cuts) > 0:
        array = block_levels(own_key, dims, cuts, -0.22, 0.18) * array
    return jnp.clip(array, min=-most, max=most).astype(held_as)


def setup_inputs(seed: int = 0) -> dict:
    key_list = jax.random.split(jax.random.key(seed), 4)
    smoother_gains = draw_smoother_gains(jax.random.fold_in(key_list[3], 71), 0)
    smoother_offsets = noise(key_list[1], (STEPS, NS), 1.0, 6.0, ((0, 4), (1, 8)))
    smoother_covs = draw_smoother_covs(jax.random.fold_in(key_list[3], 71), 0)
    return dict(smoother_gains=smoother_gains, smoother_offsets=smoother_offsets, smoother_covs=smoother_covs)


def reference(smoother_gains, smoother_offsets, smoother_covs):
    mean_now = smoother_offsets[STEPS - 1]
    cov_now = smoother_covs[STEPS - 1]
    mean_list = [mean_now]
    cov_list = [cov_now]
    for step_back in range(STEPS - 2, -1, -1):
        left_gain = smoother_gains[step_back]
        mean_sum = jnp.dot(left_gain, mean_now, preferred_element_type=jnp.float32)
        mean_now = (mean_sum + smoother_offsets[step_back].astype(jnp.float32)).astype(jnp.bfloat16)
        left_times = jnp.dot(left_gain, cov_now, preferred_element_type=jnp.float32).astype(jnp.bfloat16)
        product_full = lax.dot_general(left_times, left_gain, (((1,), (1,)), ((), ())), preferred_element_type=jnp.float32)
        cov_now = (product_full + smoother_covs[step_back].astype(jnp.float32)).astype(jnp.bfloat16)
        mean_list.append(mean_now)
        cov_list.append(cov_now)
    return (jnp.stack(mean_list[::-1]), jnp.stack(cov_list[::-1]))
```

```python
import functools

import jax
import jax.numpy as jnp
from jax import lax
from jax.experimental import pallas as pl
from jax.experimental.pallas import tpu as pltpu
from jax.sharding import PartitionSpec as P

MESH = pl.DeviceIdType.MESH
CHUNKS = 3
GROUPS = 4
PAD = 16
CONTRACT_LAST = (((1,), (1,)), ((), ()))


def ring_row(place, n):
    side = place // (n // 2)
    return (1 - side) * 2 * place + side * (2 * (n - 1 - place) + 1)


def ring_place(row, n):
    odd = row % 2
    return (1 - odd) * (row // 2) + odd * (n - 1 - row // 2)


def kernel(
    steps, n, gain_in, offset_in, cov_in, mean_out, cov_out,
    gain, cov_next, left_out, left_in, left, offsets, mean_next, mean_send,
    gain_sem, ring_send, ring_recv, left_send, left_recv,
    offset_send, offset_recv, cov_send, cov_recv, mean_sems, gate,
):
    t = lax.axis_index("tm")
    r = lax.axis_index("rows")
    place = ring_place(r, n)
    rows, size = cov_in.shape
    half = rows // 2
    piece = half // CHUNKS
    part = size // GROUPS
    per = n // GROUPS
    last = steps - 1
    right = ring_row((place + 1) % n, n)
    back = ring_row((place + n - 1) % n, n)

    def aligned(x, m):
        return pl.multiple_of(x, m)

    own_gain = pltpu.make_async_copy(
        gain_in, gain.at[pl.ds(aligned(r * rows, rows), rows), :], gain_sem
    )
    own_gain.start()

    barrier = pltpu.get_barrier_semaphore()

    def greet(i, carry):
        other = ring_row((place + i) % n, n)
        pl.semaphore_signal(barrier, inc=1, device_id=(t, other), device_id_type=MESH)
        return carry

    lax.fori_loop(1, n, greet, 0)

    @pl.when(t > 0)
    def _():
        pl.semaphore_signal(barrier, inc=1, device_id=(t - 1, r), device_id_type=MESH)

    @pl.when(t < last)
    def _():
        pl.semaphore_signal(barrier, inc=1, device_id=(t + 1, r), device_id_type=MESH)

    pl.semaphore_wait(barrier, n - 1 + (t + last - 1) // last + (2 * last - t - 1) // last)

    def cov_copy(source, j):
        columns = pl.ds(aligned(j * part, part), part)
        return pltpu.make_async_remote_copy(
            src_ref=source.at[:, columns],
            dst_ref=cov_next.at[:, columns],
            send_sem=cov_send.at[j],
            recv_sem=cov_recv.at[j],
            device_id=(t - 1, r),
            device_id_type=MESH,
        )

    def mean_copy():
        return pltpu.make_async_remote_copy(
            src_ref=mean_send,
            dst_ref=mean_next,
            send_sem=mean_sems.at[0],
            recv_sem=mean_sems.at[1],
            device_id=(t - 1, r),
            device_id_type=MESH,
        )

    def offset_copy(i):
        other = ring_row((place + i) % n, n)
        return pltpu.make_async_remote_copy(
            src_ref=offset_in,
            dst_ref=offsets.at[r],
            send_sem=offset_send.at[i],
            recv_sem=offset_recv.at[r],
            device_id=(t, other),
            device_id_type=MESH,
        )

    def offset_arrival(i):
        other = ring_row((place + i) % n, n)
        return pltpu.make_async_remote_copy(
            src_ref=offset_in,
            dst_ref=offsets.at[other],
            send_sem=offset_send.at[i],
            recv_sem=offset_recv.at[other],
            device_id=(t, other),
            device_id_type=MESH,
        )

    def ring_copy(way, hop, c):
        origin = ring_row((place + (n - hop if way == 0 else hop)) % n, n)
        span = pl.ds(aligned(origin * rows + way * half + c * piece, piece), piece)
        return pltpu.make_async_remote_copy(
            src_ref=gain.at[span, :],
            dst_ref=gain.at[span, :],
            send_sem=ring_send.at[way, hop, c],
            recv_sem=ring_recv.at[way, hop, c],
            device_id=(t, right if way == 0 else back),
            device_id_type=MESH,
        )

    def ring_arrival(way, hop, c):
        origin = ring_row((place + (n - 1 - hop if way == 0 else hop + 1)) % n, n)
        span = pl.ds(aligned(origin * rows + way * half + c * piece, piece), piece)
        return pltpu.make_async_remote_copy(
            src_ref=gain.at[span, :],
            dst_ref=gain.at[span, :],
            send_sem=ring_send.at[way, hop, c],
            recv_sem=ring_recv.at[way, hop, c],
            device_id=(t, right if way == 0 else back),
            device_id_type=MESH,
        )

    def left_copy(d, way):
        span = pl.ds(way * half, half)
        return pltpu.make_async_remote_copy(
            src_ref=left_out.at[d, span, :],
            dst_ref=left_in.at[r, span, :],
            send_sem=left_send.at[way, d],
            recv_sem=left_recv.at[way, r],
            device_id=(t, d),
            device_id_type=MESH,
        )

    def left_arrival(d, way):
        span = pl.ds(way * half, half)
        return pltpu.make_async_remote_copy(
            src_ref=left_out.at[d, span, :],
            dst_ref=left_in.at[d, span, :],
            send_sem=left_send.at[way, d],
            recv_sem=left_recv.at[way, d],
            device_id=(t, d),
            device_id_type=MESH,
        )

    def await_cov():
        for j in range(GROUPS):
            cov_copy(cov_in, j).wait_recv()

    @pl.when(t == last)
    def _():
        for j in range(GROUPS):
            cov_copy(cov_in, j).start()

    def send_offset(i, carry):
        offset_copy(i).start()
        return carry

    lax.fori_loop(1, n, send_offset, 0)
    own_gain.wait()

    def left_half(d, way):
        block = gain[pl.ds(aligned(d * rows + way * half, half), half), :]
        product = lax.dot_general(
            block, cov_next[...], CONTRACT_LAST, preferred_element_type=jnp.float32
        )
        return product.astype(jnp.bfloat16)

    @pl.when(t < last)
    def _():
        @pl.when(t % 2 == 0)
        def _():
            @pl.when(t < last - 1)
            def _():
                pl.semaphore_wait(gate, 1)

        for c in range(CHUNKS):
            for way in range(2):
                ring_copy(way, 0, c).start()

        @pl.when(t == last - 1)
        def _():
            await_cov()
            for way in range(2):
                left_in[r, pl.ds(way * half, half), :] = left_half(r, way)

        def pass_on(hop, carry):
            for c in range(CHUNKS):
                for way in range(2):
                    ring_arrival(way, hop - 1, c).wait_recv()
                    ring_copy(way, hop, c).start()

            @pl.when(t == last - 1)
            def _():
                for way in range(2):
                    d = ring_row((place + (n - hop if way == 0 else hop)) % n, n)
                    left_out[d, pl.ds(way * half, half), :] = left_half(d, way)
                    left_copy(d, way).start()

            return carry

        lax.fori_loop(1, n - 1, pass_on, 0)

        for c in range(CHUNKS):
            for way in range(2):
                ring_arrival(way, n - 2, c).wait_recv()

        @pl.when(t % 2 == 1)
        def _():
            pl.semaphore_signal(gate, inc=1, device_id=(t - 1, r), device_id_type=MESH)

        @pl.when(t == last - 1)
        def _():
            for way in range(2):
                d = ring_row((place + (1 if way == 0 else n - 1)) % n, n)
                left_out[d, pl.ds(way * half, half), :] = left_half(d, way)
                left_copy(d, way).start()

    offsets[r] = offset_in[...]

    def await_offset(i, carry):
        offset_arrival(i).wait_recv()
        return carry

    lax.fori_loop(1, n, await_offset, 0)
    whole_offset = offsets[0]
    for i in range(1, n):
        whole_offset = whole_offset + offsets[i]

    @pl.when(t == last)
    def _():
        mean_send[...] = whole_offset
        mean_copy().start()
        mean_out[...] = whole_offset
        cov_out[...] = cov_in[...]

    @pl.when(t < last)
    def _():
        @pl.when(t < last - 1)
        def _():
            await_cov()

            def left_part(j, carry):
                g = (r // per + 1 + j) % GROUPS
                block = gain[pl.ds(aligned(g * part, part), part), :]
                product = lax.dot_general(
                    block, cov_next[...], CONTRACT_LAST, preferred_element_type=jnp.float32
                ).astype(jnp.bfloat16)
                for i in range(per):
                    d = g * per + i
                    left_out[d] = product[i * rows:(i + 1) * rows]

                    @pl.when(d != r)
                    def _():
                        for way in range(2):
                            left_copy(d, way).start()

                    @pl.when(d == r)
                    def _():
                        left_in[r] = product[i * rows:(i + 1) * rows]

                return carry

            lax.fori_loop(0, GROUPS, left_part, 0)

        mean_copy().wait_recv()
        left[rows:, :] = jnp.broadcast_to(mean_next[...], (PAD, size)).astype(jnp.bfloat16)

        def await_left(i, carry):
            for way in range(2):
                left_arrival(ring_row((place + i) % n, n), way).wait_recv()
            return carry

        lax.fori_loop(1, n, await_left, 0)
        for d in range(n):
            left[0:rows, d * rows:(d + 1) * rows] = left_in[d]

        offsets[0] = whole_offset

        def right_part(j, carry):
            columns = pl.ds(aligned(j * part, part), part)
            product = lax.dot_general(
                left[...], gain[columns, :], CONTRACT_LAST, preferred_element_type=jnp.float32
            )
            cov_out[:, columns] = (
                product[:rows] + cov_in[:, columns].astype(jnp.float32)
            ).astype(jnp.bfloat16)
            mean = product[rows:rows + 1] + offsets[0, :, columns]
            mean_send[:, columns] = mean.astype(jnp.bfloat16).astype(jnp.float32)

            @pl.when(t > 0)
            def _():
                cov_copy(cov_out, j).start()

            return carry

        lax.fori_loop(0, GROUPS, right_part, 0)
        mean_out[...] = mean_send[...]

        @pl.when(t > 0)
        def _():
            mean_copy().start()

        def left_gone(i, carry):
            for way in range(2):
                left_copy(ring_row((place + i) % n, n), way).wait_send()
            return carry

        lax.fori_loop(1, n, left_gone, 0)

        def ring_gone(hop, carry):
            for c in range(CHUNKS):
                for way in range(2):
                    ring_copy(way, hop, c).wait_send()
            return carry

        lax.fori_loop(0, n - 1, ring_gone, 0)

    @pl.when(t > 0)
    def _():
        for j in range(GROUPS):
            cov_copy(cov_out, j).wait_send()
        mean_copy().wait_send()

    def offset_gone(i, carry):
        offset_copy(i).wait_send()
        return carry

    lax.fori_loop(1, n, offset_gone, 0)


def shards(steps, n, smoother_gains, smoother_offsets, smoother_covs):
    own_gain = smoother_gains[0]
    own_cov = smoother_covs[0]
    rows, size = own_cov.shape
    start = lax.axis_index("rows") * rows
    offset_row = lax.dynamic_update_slice(
        jnp.zeros((1, size), jnp.float32), smoother_offsets.astype(jnp.float32), (0, start)
    )
    vmem = pl.BlockSpec(memory_space=pltpu.VMEM)
    dma = pltpu.SemaphoreType.DMA
    mean_row, cov = pl.pallas_call(
        functools.partial(kernel, steps, n),
        out_shape=(
            jax.ShapeDtypeStruct((1, size), jnp.float32),
            jax.ShapeDtypeStruct((rows, size), jnp.bfloat16),
        ),
        in_specs=[pl.BlockSpec(memory_space=pl.ANY), vmem, vmem],
        out_specs=(vmem, vmem),
        scratch_shapes=[
            pltpu.VMEM((size, size), jnp.bfloat16),
            pltpu.VMEM((rows, size), jnp.bfloat16),
            pltpu.VMEM((n, rows, rows), jnp.bfloat16),
            pltpu.VMEM((n, rows, rows), jnp.bfloat16),
            pltpu.VMEM((rows + PAD, size), jnp.bfloat16),
            pltpu.VMEM((n, 1, size), jnp.float32),
            pltpu.VMEM((1, size), jnp.float32),
            pltpu.VMEM((1, size), jnp.float32),
            dma,
            dma((2, n, CHUNKS)),
            dma((2, n, CHUNKS)),
            dma((2, n)),
            dma((2, n)),
            dma((n,)),
            dma((n,)),
            dma((GROUPS,)),
            dma((GROUPS,)),
            dma((2,)),
            pltpu.SemaphoreType.REGULAR,
        ],
        compiler_params=pltpu.CompilerParams(
            collective_id=0, has_side_effects=True, vmem_limit_bytes=40 << 20
        ),
    )(own_gain, offset_row, own_cov)
    mean = lax.dynamic_slice(mean_row, (0, start), (1, rows)).astype(jnp.bfloat16)
    return mean, cov[None]


def solution(mesh):
    in_specs = (P("tm", "rows", None), P("tm", "rows"), P("tm", "rows", None))
    out_specs = (P("tm", "rows"), P("tm", "rows", None))
    body = functools.partial(shards, mesh.shape["tm"], mesh.shape["rows"])
    return jax.shard_map(body, mesh=mesh, in_specs=in_specs, out_specs=out_specs, check_vma=False)
```

```python
import functools

import jax
import jax.numpy as jnp
from jax import lax
from jax.experimental import pallas as pl
from jax.experimental.pallas import tpu as pltpu
from jax.sharding import PartitionSpec as P

MESH = pl.DeviceIdType.MESH
CHUNKS = 3
GROUPS = 4
LEFT_GROUPS = 2
HEAD_START = 2
PAD = 16
CONTRACT_LAST = (((1,), (1,)), ((), ()))


def ring_row(place, n):
    side = place // (n // 2)
    return (1 - side) * 2 * place + side * (2 * (n - 1 - place) + 1)


def ring_place(row, n):
    odd = row % 2
    return (1 - odd) * (row // 2) + odd * (n - 1 - row // 2)


def main_lanes(rows):
    return 128 if rows == 192 else rows


def kernel(
    steps, n, gain_in, offset_in, cov_hbm, mean_out, cov_hbm_out,
    gain, cov_in, cov_out, cov_next, left_out, left_in, left, offsets, mean_next, mean_send,
    gain_sem, ring_send, ring_recv, left_send, left_recv,
    offset_send, offset_recv, cov_send, cov_recv, mean_sems, cov_sem, out_sem, gate,
):
    t = lax.axis_index("tm")
    r = lax.axis_index("rows")
    place = ring_place(r, n)
    rows, size = cov_in.shape
    half = rows // 2
    piece = half // CHUNKS
    part = size // GROUPS
    left_part_rows = size // LEFT_GROUPS
    per = n // LEFT_GROUPS
    last = steps - 1
    right = ring_row((place + 1) % n, n)
    back = ring_row((place + n - 1) % n, n)

    def aligned(x, m):
        return pl.multiple_of(x, m)

    own_gain = pltpu.make_async_copy(
        gain_in, gain.at[pl.ds(aligned(r * rows, rows), rows), :], gain_sem
    )
    own_gain.start()
    own_cov = pltpu.make_async_copy(cov_hbm, cov_in, cov_sem)
    own_cov.start()

    def store_cov(j):
        columns = pl.ds(aligned(j * part, part), part)
        return pltpu.make_async_copy(
            cov_out.at[:, columns], cov_hbm_out.at[:, columns], out_sem.at[j]
        )

    def store_block(ref, index, way, block):
        main = main_lanes(rows)
        ref[index, way, 0:half, :] = block[:, :main]
        if main < rows:
            for i in range(2):
                ref[index, way, half:, i * 64:(i + 1) * 64] = block[
                    i * half // 2:(i + 1) * half // 2, main:
                ]

    def place_block(d, way):
        main = main_lanes(rows)
        top, at = way * half, d * rows
        left[top:top + half, at:at + main] = left_in[d, way, 0:half, :]
        if main < rows:
            for i in range(2):
                left[top + i * half // 2:top + (i + 1) * half // 2, at + main:at + rows] = (
                    left_in[d, way, half:, i * 64:(i + 1) * 64]
                )

    barrier = pltpu.get_barrier_semaphore()

    def greet(i, carry):
        other = ring_row((place + i) % n, n)
        pl.semaphore_signal(barrier, inc=1, device_id=(t, other), device_id_type=MESH)
        return carry

    lax.fori_loop(1, n, greet, 0)

    @pl.when(t > 0)
    def _():
        pl.semaphore_signal(barrier, inc=1, device_id=(t - 1, r), device_id_type=MESH)

    @pl.when(t < last)
    def _():
        pl.semaphore_signal(barrier, inc=1, device_id=(t + 1, r), device_id_type=MESH)

    pl.semaphore_wait(barrier, n - 1 + (t + last - 1) // last + (2 * last - t - 1) // last)

    def cov_copy(source, j):
        columns = pl.ds(aligned(j * part, part), part)
        return pltpu.make_async_remote_copy(
            src_ref=source.at[:, columns],
            dst_ref=cov_next.at[:, columns],
            send_sem=cov_send.at[j],
            recv_sem=cov_recv.at[j],
            device_id=(t - 1, r),
            device_id_type=MESH,
        )

    def mean_copy():
        return pltpu.make_async_remote_copy(
            src_ref=mean_send,
            dst_ref=mean_next,
            send_sem=mean_sems.at[0],
            recv_sem=mean_sems.at[1],
            device_id=(t - 1, r),
            device_id_type=MESH,
        )

    def offset_copy(i):
        other = ring_row((place + i) % n, n)
        return pltpu.make_async_remote_copy(
            src_ref=offset_in,
            dst_ref=offsets.at[r],
            send_sem=offset_send.at[i],
            recv_sem=offset_recv.at[r],
            device_id=(t, other),
            device_id_type=MESH,
        )

    def offset_arrival(i):
        other = ring_row((place + i) % n, n)
        return pltpu.make_async_remote_copy(
            src_ref=offset_in,
            dst_ref=offsets.at[other],
            send_sem=offset_send.at[i],
            recv_sem=offset_recv.at[other],
            device_id=(t, other),
            device_id_type=MESH,
        )

    def ring_copy(way, hop, c):
        origin = ring_row((place + (n - hop if way == 0 else hop)) % n, n)
        span = pl.ds(aligned(origin * rows + way * half + c * piece, piece), piece)
        return pltpu.make_async_remote_copy(
            src_ref=gain.at[span, :],
            dst_ref=gain.at[span, :],
            send_sem=ring_send.at[way, hop, c],
            recv_sem=ring_recv.at[way, hop, c],
            device_id=(t, right if way == 0 else back),
            device_id_type=MESH,
        )

    def ring_arrival(way, hop, c):
        origin = ring_row((place + (n - 1 - hop if way == 0 else hop + 1)) % n, n)
        span = pl.ds(aligned(origin * rows + way * half + c * piece, piece), piece)
        return pltpu.make_async_remote_copy(
            src_ref=gain.at[span, :],
            dst_ref=gain.at[span, :],
            send_sem=ring_send.at[way, hop, c],
            recv_sem=ring_recv.at[way, hop, c],
            device_id=(t, right if way == 0 else back),
            device_id_type=MESH,
        )

    def left_copy(d, way):
        return pltpu.make_async_remote_copy(
            src_ref=left_out.at[d, way],
            dst_ref=left_in.at[r, way],
            send_sem=left_send.at[way, d],
            recv_sem=left_recv.at[way, r],
            device_id=(t, d),
            device_id_type=MESH,
        )

    def left_arrival(d, way):
        return pltpu.make_async_remote_copy(
            src_ref=left_out.at[d, way],
            dst_ref=left_in.at[d, way],
            send_sem=left_send.at[way, d],
            recv_sem=left_recv.at[way, d],
            device_id=(t, d),
            device_id_type=MESH,
        )

    def await_cov():
        for j in range(GROUPS):
            cov_copy(cov_in, j).wait_recv()

    own_cov.wait()

    @pl.when(t == last)
    def _():
        for j in range(GROUPS):
            cov_copy(cov_in, j).start()

    def send_offset(i, carry):
        offset_copy(i).start()
        return carry

    lax.fori_loop(1, n, send_offset, 0)
    own_gain.wait()

    def left_half(d, way):
        block = gain[pl.ds(aligned(d * rows + way * half, half), half), :]
        product = lax.dot_general(
            block, cov_next[...], CONTRACT_LAST, preferred_element_type=jnp.float32
        )
        return product.astype(jnp.bfloat16)

    @pl.when(t < last)
    def _():
        @pl.when(t % 2 == 0)
        def _():
            @pl.when(t < last - 1)
            def _():
                pl.semaphore_wait(gate, 1)

        for c in range(CHUNKS):
            for way in range(2):
                ring_copy(way, 0, c).start()

        @pl.when(t == last - 1)
        def _():
            await_cov()
            for way in range(2):
                store_block(left_in, r, way, left_half(r, way))

        def pass_on(hop, carry):
            for c in range(CHUNKS):
                for way in range(2):
                    ring_arrival(way, hop - 1, c).wait_recv()
                    ring_copy(way, hop, c).start()

            @pl.when(hop == min(HEAD_START, n - 2))
            def _():
                @pl.when(t % 2 == 1)
                def _():
                    pl.semaphore_signal(gate, inc=1, device_id=(t - 1, r), device_id_type=MESH)

            @pl.when(t == last - 1)
            def _():
                for way in range(2):
                    d = ring_row((place + (n - hop if way == 0 else hop)) % n, n)
                    store_block(left_out, d, way, left_half(d, way))
                    left_copy(d, way).start()

            return carry

        lax.fori_loop(1, n - 1, pass_on, 0)

        for c in range(CHUNKS):
            for way in range(2):
                ring_arrival(way, n - 2, c).wait_recv()

        @pl.when(t == last - 1)
        def _():
            for way in range(2):
                d = ring_row((place + (1 if way == 0 else n - 1)) % n, n)
                store_block(left_out, d, way, left_half(d, way))
                left_copy(d, way).start()

    offsets[r] = offset_in[...]

    def await_offset(i, carry):
        offset_arrival(i).wait_recv()
        return carry

    lax.fori_loop(1, n, await_offset, 0)
    whole_offset = offsets[0]
    for i in range(1, n):
        whole_offset = whole_offset + offsets[i]

    @pl.when(t == last)
    def _():
        mean_send[...] = whole_offset
        mean_copy().start()
        mean_out[...] = whole_offset
        keep = pltpu.make_async_copy(cov_in, cov_hbm_out, cov_sem)
        keep.start()
        keep.wait()

    @pl.when(t < last)
    def _():
        @pl.when(t < last - 1)
        def _():
            await_cov()

            def left_part(j, carry):
                g = (r // per + 1 + j) % LEFT_GROUPS
                span = pl.ds(aligned(g * left_part_rows, left_part_rows), left_part_rows)
                product = lax.dot_general(
                    gain[span, :], cov_next[...], CONTRACT_LAST,
                    preferred_element_type=jnp.float32,
                ).astype(jnp.bfloat16)
                for i in range(per):
                    d = g * per + i
                    for way in range(2):
                        top = i * rows + way * half
                        store_block(left_out, d, way, product[top:top + half])

                def send(i, carry):
                    d = g * per + (r + i) % per

                    @pl.when(d != r)
                    def _():
                        for way in range(2):
                            left_copy(d, way).start()

                    return carry

                lax.fori_loop(0, per, send, 0)
                return carry

            lax.fori_loop(0, LEFT_GROUPS, left_part, 0)
            left_in[r] = left_out[r]

        mean_copy().wait_recv()
        left[rows:, :] = jnp.broadcast_to(mean_next[...], (PAD, size)).astype(jnp.bfloat16)

        def await_left(i, carry):
            for way in range(2):
                left_arrival(ring_row((place + i) % n, n), way).wait_recv()
            return carry

        lax.fori_loop(1, n, await_left, 0)
        for d in range(n):
            for way in range(2):
                place_block(d, way)

        offsets[0] = whole_offset

        def right_part(j, carry):
            columns = pl.ds(aligned(j * part, part), part)
            product = lax.dot_general(
                left[...], gain[columns, :], CONTRACT_LAST, preferred_element_type=jnp.float32
            )
            cov_out[:, columns] = (
                product[:rows] + cov_in[:, columns].astype(jnp.float32)
            ).astype(jnp.bfloat16)
            mean = product[rows:rows + 1] + offsets[0, :, columns]
            mean_send[:, columns] = mean.astype(jnp.bfloat16).astype(jnp.float32)

            @pl.when(t > 0)
            def _():
                cov_copy(cov_out, j).start()

            store_cov(j).start()
            return carry

        lax.fori_loop(0, GROUPS, right_part, 0)
        mean_out[...] = mean_send[...]

        @pl.when(t > 0)
        def _():
            mean_copy().start()

        for j in range(GROUPS):
            store_cov(j).wait()

        def left_gone(i, carry):
            for way in range(2):
                left_copy(ring_row((place + i) % n, n), way).wait_send()
            return carry

        lax.fori_loop(1, n, left_gone, 0)

        def ring_gone(hop, carry):
            for c in range(CHUNKS):
                for way in range(2):
                    ring_copy(way, hop, c).wait_send()
            return carry

        lax.fori_loop(0, n - 1, ring_gone, 0)

    @pl.when(t > 0)
    def _():
        for j in range(GROUPS):
            cov_copy(cov_out, j).wait_send()
        mean_copy().wait_send()

    def offset_gone(i, carry):
        offset_copy(i).wait_send()
        return carry

    lax.fori_loop(1, n, offset_gone, 0)


def shards(steps, n, smoother_gains, smoother_offsets, smoother_covs):
    own_gain = smoother_gains[0]
    own_cov = smoother_covs[0]
    rows, size = own_cov.shape
    start = lax.axis_index("rows") * rows
    offset_row = lax.dynamic_update_slice(
        jnp.zeros((1, size), jnp.float32), smoother_offsets.astype(jnp.float32), (0, start)
    )
    vmem = pl.BlockSpec(memory_space=pltpu.VMEM)
    hbm = pl.BlockSpec(memory_space=pl.ANY)
    lanes = main_lanes(rows)
    folded = (n, 2, rows // 2 * rows // lanes, lanes)
    dma = pltpu.SemaphoreType.DMA
    mean_row, cov = pl.pallas_call(
        functools.partial(kernel, steps, n),
        out_shape=(
            jax.ShapeDtypeStruct((1, size), jnp.float32),
            jax.ShapeDtypeStruct((rows, size), jnp.bfloat16),
        ),
        in_specs=[hbm, vmem, hbm],
        out_specs=(vmem, hbm),
        scratch_shapes=[
            pltpu.VMEM((size, size), jnp.bfloat16),
            pltpu.VMEM((rows, size), jnp.bfloat16),
            pltpu.VMEM((rows, size), jnp.bfloat16),
            pltpu.VMEM((rows, size), jnp.bfloat16),
            pltpu.VMEM(folded, jnp.bfloat16),
            pltpu.VMEM(folded, jnp.bfloat16),
            pltpu.VMEM((rows + PAD, size), jnp.bfloat16),
            pltpu.VMEM((n, 1, size), jnp.float32),
            pltpu.VMEM((1, size), jnp.float32),
            pltpu.VMEM((1, size), jnp.float32),
            dma,
            dma((2, n, CHUNKS)),
            dma((2, n, CHUNKS)),
            dma((2, n)),
            dma((2, n)),
            dma((n,)),
            dma((n,)),
            dma((GROUPS,)),
            dma((GROUPS,)),
            dma((2,)),
            dma,
            dma((GROUPS,)),
            pltpu.SemaphoreType.REGULAR,
        ],
        compiler_params=pltpu.CompilerParams(
            collective_id=0, has_side_effects=True, vmem_limit_bytes=62 << 20
        ),
    )(own_gain, offset_row, own_cov)
    mean = lax.dynamic_slice(mean_row, (0, start), (1, rows)).astype(jnp.bfloat16)
    return mean, cov[None]


def solution(mesh):
    in_specs = (P("tm", "rows", None), P("tm", "rows"), P("tm", "rows", None))
    out_specs = (P("tm", "rows"), P("tm", "rows", None))
    body = functools.partial(shards, mesh.shape["tm"], mesh.shape["rows"])
    return jax.shard_map(body, mesh=mesh, in_specs=in_specs, out_specs=out_specs, check_vma=False)
```

```python
import functools

import jax
import jax.numpy as jnp
from jax import lax
from jax.experimental import pallas as pl
from jax.experimental.pallas import tpu as pltpu
from jax.sharding import PartitionSpec as P

MESH = pl.DeviceIdType.MESH
PIECES = 6
THIRDS = 3
GROUPS = 4
LEFT_GROUPS = 2
HEAD_START = 4
PAD = 16
CONTRACT_LAST = (((1,), (1,)), ((), ()))


def ring_row(place, n):
    side = place // (n // 2)
    return (1 - side) * 2 * place + side * (2 * (n - 1 - place) + 1)


def ring_place(row, n):
    odd = row % 2
    return (1 - odd) * (row // 2) + odd * (n - 1 - row // 2)


def main_lanes(rows):
    return 128 if rows == 192 else rows


def kernel(
    steps, n, gain_in, offset_in, cov_hbm, mean_out, cov_hbm_out,
    gain, cov_in, cov_out, cov_next, left_out, left_in, left, offsets, mean_next, mean_send,
    gain_sem, ring_send, ring_recv, left_send, left_recv,
    offset_send, offset_recv, cov_send, cov_recv, mean_sems, cov_sem, out_sem,
    relay, seed_send, seed_recv, relay_send, relay_recv, back_send, back_recv, gate,
):
    t = lax.axis_index("tm")
    r = lax.axis_index("rows")
    place = ring_place(r, n)
    rows, size = cov_in.shape
    third = rows // THIRDS
    piece = rows // PIECES
    part = size // GROUPS
    left_part_rows = size // LEFT_GROUPS
    per = n // LEFT_GROUPS
    last = steps - 1
    first = last - 1
    helper = last - 3
    right = ring_row((place + 1) % n, n)
    back = ring_row((place + n - 1) % n, n)

    def aligned(x, m):
        return pl.multiple_of(x, m)

    own_gain = pltpu.make_async_copy(
        gain_in, gain.at[r], gain_sem
    )
    own_gain.start()
    own_cov = pltpu.make_async_copy(cov_hbm, cov_in, cov_sem)
    own_cov.start()

    def store_cov(j):
        columns = pl.ds(aligned(j * part, part), part)
        return pltpu.make_async_copy(
            cov_out.at[:, columns], cov_hbm_out.at[:, columns], out_sem.at[j]
        )

    def store_block(ref, index, way, block):
        main = main_lanes(rows)
        ref[index, way, 0:third, :] = block[:, :main]
        if main < rows:
            for i in range(2):
                ref[index, way, third:, i * 64:(i + 1) * 64] = block[
                    i * third // 2:(i + 1) * third // 2, main:
                ]

    def place_block(d, way):
        main = main_lanes(rows)
        top, at = way * third, d * rows
        left[top:top + third, at:at + main] = left_in[d, way, 0:third, :]
        if main < rows:
            for i in range(2):
                left[top + i * third // 2:top + (i + 1) * third // 2, at + main:at + rows] = (
                    left_in[d, way, third:, i * 64:(i + 1) * 64]
                )

    barrier = pltpu.get_barrier_semaphore()

    def greet(i, carry):
        other = ring_row((place + i) % n, n)
        pl.semaphore_signal(barrier, inc=1, device_id=(t, other), device_id_type=MESH)
        return carry

    lax.fori_loop(1, n, greet, 0)

    @pl.when(t > 0)
    def _():
        pl.semaphore_signal(barrier, inc=1, device_id=(t - 1, r), device_id_type=MESH)

    @pl.when(t < last)
    def _():
        pl.semaphore_signal(barrier, inc=1, device_id=(t + 1, r), device_id_type=MESH)

    @pl.when(t == first)
    def _():
        pl.semaphore_signal(barrier, inc=1, device_id=(helper, r), device_id_type=MESH)

    @pl.when(t == helper)
    def _():
        pl.semaphore_signal(barrier, inc=1, device_id=(first, r), device_id_type=MESH)

    def same(x, y):
        square = steps * steps
        return 1 - ((x - y) * (x - y) + square - 1) // square

    greetings = n + 1 - same(t, 0) - same(t, last) + same(t, first) + same(t, helper)
    pl.semaphore_wait(barrier, greetings)

    def cov_copy(source, j):
        columns = pl.ds(aligned(j * part, part), part)
        return pltpu.make_async_remote_copy(
            src_ref=source.at[:, columns],
            dst_ref=cov_next.at[:, columns],
            send_sem=cov_send.at[j],
            recv_sem=cov_recv.at[j],
            device_id=(t - 1, r),
            device_id_type=MESH,
        )

    def mean_copy():
        return pltpu.make_async_remote_copy(
            src_ref=mean_send,
            dst_ref=mean_next,
            send_sem=mean_sems.at[0],
            recv_sem=mean_sems.at[1],
            device_id=(t - 1, r),
            device_id_type=MESH,
        )

    def offset_copy(i):
        other = ring_row((place + i) % n, n)
        return pltpu.make_async_remote_copy(
            src_ref=offset_in,
            dst_ref=offsets.at[r],
            send_sem=offset_send.at[i],
            recv_sem=offset_recv.at[r],
            device_id=(t, other),
            device_id_type=MESH,
        )

    def offset_arrival(i):
        other = ring_row((place + i) % n, n)
        return pltpu.make_async_remote_copy(
            src_ref=offset_in,
            dst_ref=offsets.at[other],
            send_sem=offset_send.at[i],
            recv_sem=offset_recv.at[other],
            device_id=(t, other),
            device_id_type=MESH,
        )

    def sent_origin(way, hop):
        return ring_row((place + (n - hop if way == 0 else hop)) % n, n)

    def ring_part(origin, way, hop, c, chunks):
        span = pl.ds((way * chunks + c) * piece, piece)
        return pltpu.make_async_remote_copy(
            src_ref=gain.at[origin, span, :],
            dst_ref=gain.at[origin, span, :],
            send_sem=ring_send.at[way, hop, c],
            recv_sem=ring_recv.at[way, hop, c],
            device_id=(t, right if way == 0 else back),
            device_id_type=MESH,
        )

    def ring_copy(way, hop, c, chunks):
        return ring_part(sent_origin(way, hop), way, hop, c, chunks)

    def ring_arrival(way, hop, c, chunks):
        return ring_part(sent_origin(way, hop + 1), way, hop, c, chunks)

    def seed_copy(way):
        return pltpu.make_async_remote_copy(
            src_ref=gain.at[r, pl.ds((4 + way) * piece, piece), :],
            dst_ref=relay.at[r, way],
            send_sem=seed_send.at[way],
            recv_sem=seed_recv.at[way],
            device_id=(helper, r),
            device_id_type=MESH,
        )

    def relay_part(origin, way, hop):
        return pltpu.make_async_remote_copy(
            src_ref=relay.at[origin, way],
            dst_ref=relay.at[origin, way],
            send_sem=relay_send.at[way, hop],
            recv_sem=relay_recv.at[way, hop],
            device_id=(t, right if way == 0 else back),
            device_id_type=MESH,
        )

    def relay_copy(way, hop):
        return relay_part(sent_origin(way, hop), way, hop)

    def relay_arrival(way, hop):
        return relay_part(sent_origin(way, hop + 1), way, hop)

    def back_copy(way, hop):
        origin = sent_origin(way, hop + 1)
        return pltpu.make_async_remote_copy(
            src_ref=relay.at[origin, way],
            dst_ref=gain.at[origin, pl.ds((4 + way) * piece, piece), :],
            send_sem=back_send.at[way, hop],
            recv_sem=back_recv.at[way, hop],
            device_id=(first, r),
            device_id_type=MESH,
        )

    def left_copy(d, way):
        return pltpu.make_async_remote_copy(
            src_ref=left_out.at[d, way],
            dst_ref=left_in.at[r, way],
            send_sem=left_send.at[way, d],
            recv_sem=left_recv.at[way, r],
            device_id=(t, d),
            device_id_type=MESH,
        )

    def left_arrival(d, way):
        return pltpu.make_async_remote_copy(
            src_ref=left_out.at[d, way],
            dst_ref=left_in.at[d, way],
            send_sem=left_send.at[way, d],
            recv_sem=left_recv.at[way, d],
            device_id=(t, d),
            device_id_type=MESH,
        )

    def await_cov():
        for j in range(GROUPS):
            cov_copy(cov_in, j).wait_recv()

    own_cov.wait()

    @pl.when(t == last)
    def _():
        for j in range(GROUPS):
            cov_copy(cov_in, j).start()

    def send_offset(i, carry):
        offset_copy(i).start()
        return carry

    lax.fori_loop(1, n, send_offset, 0)
    own_gain.wait()

    def left_third(d, way):
        product = lax.dot_general(
            gain[d, pl.ds(way * third, third), :], cov_next[...], CONTRACT_LAST,
            preferred_element_type=jnp.float32,
        )
        return product.astype(jnp.bfloat16)

    def send_third(d, way):
        store_block(left_out, d, way, left_third(d, way))
        left_copy(d, way).start()

    def go_round(chunks, begin, between):
        for c in range(chunks):
            for way in range(2):
                ring_copy(way, 0, c, chunks).start()
        begin()

        def pass_on(hop, carry):
            for c in range(chunks):
                for way in range(2):
                    ring_arrival(way, hop - 1, c, chunks).wait_recv()
                    ring_copy(way, hop, c, chunks).start()
            between(hop)
            return carry

        lax.fori_loop(1, n - 1, pass_on, 0)
        for c in range(chunks):
            for way in range(2):
                ring_arrival(way, n - 2, c, chunks).wait_recv()

    def round_gone(chunks):
        def gone(hop, carry):
            for c in range(chunks):
                for way in range(2):
                    ring_copy(way, hop, c, chunks).wait_send()
            return carry

        lax.fori_loop(0, n - 1, gone, 0)

    @pl.when(t == first)
    def _():
        for way in range(2):
            seed_copy(way).start()

        def begin():
            await_cov()
            for way in range(THIRDS):
                store_block(left_in, r, way, left_third(r, way))

        def between(hop):
            for way in range(2):
                send_third(sent_origin(way, hop), way)

        go_round(2, begin, between)
        for way in range(2):
            send_third(sent_origin(way, n - 1), way)

        def returned(hop, carry):
            for way in range(2):
                back_copy(way, hop).wait_recv()
            return carry

        lax.fori_loop(0, n - 1, returned, 0)
        tail = gain[:, 2 * third:, :].reshape(n * third, size)
        product = lax.dot_general(
            tail, cov_next[...], CONTRACT_LAST, preferred_element_type=jnp.float32
        ).astype(jnp.bfloat16)
        for d in range(n):
            store_block(left_out, d, 2, product[d * third:(d + 1) * third])

        def send_tail(i, carry):
            left_copy(ring_row((place + i) % n, n), 2).start()
            return carry

        lax.fori_loop(1, n, send_tail, 0)
        round_gone(2)
        for way in range(2):
            seed_copy(way).wait_send()

    @pl.when(t == helper)
    def _():
        for way in range(2):
            seed_copy(way).wait_recv()
            relay_copy(way, 0).start()

        def relay_on(hop, carry):
            for way in range(2):
                relay_arrival(way, hop - 1).wait_recv()
                relay_copy(way, hop).start()
                back_copy(way, hop - 1).start()
            return carry

        lax.fori_loop(1, n - 1, relay_on, 0)
        for way in range(2):
            relay_arrival(way, n - 2).wait_recv()
            back_copy(way, n - 2).start()

    @pl.when(t < first)
    def _():
        @pl.when(t % 2 == 0)
        def _():
            pl.semaphore_wait(gate, 1)

        def begin():
            pass

        def between(hop):
            @pl.when(hop == min(HEAD_START, n - 2))
            def _():
                @pl.when(t % 2 == 1)
                def _():
                    pl.semaphore_signal(gate, inc=1, device_id=(t - 1, r), device_id_type=MESH)

        go_round(3, begin, between)
        round_gone(3)

    @pl.when(t == helper)
    def _():
        def relayed(hop, carry):
            for way in range(2):
                relay_copy(way, hop).wait_send()
                back_copy(way, hop).wait_send()
            return carry

        lax.fori_loop(0, n - 1, relayed, 0)

    offsets[r] = offset_in[...]

    def await_offset(i, carry):
        offset_arrival(i).wait_recv()
        return carry

    lax.fori_loop(1, n, await_offset, 0)
    whole_offset = offsets[0]
    for i in range(1, n):
        whole_offset = whole_offset + offsets[i]

    @pl.when(t == last)
    def _():
        mean_send[...] = whole_offset
        mean_copy().start()
        mean_out[...] = whole_offset
        keep = pltpu.make_async_copy(cov_in, cov_hbm_out, cov_sem)
        keep.start()
        keep.wait()

    @pl.when(t < last)
    def _():
        @pl.when(t < last - 1)
        def _():
            await_cov()

            def left_part(j, carry):
                g = (r // per + 1 + j) % LEFT_GROUPS
                product = lax.dot_general(
                    gain[pl.ds(g * per, per)].reshape(left_part_rows, size),
                    cov_next[...], CONTRACT_LAST,
                    preferred_element_type=jnp.float32,
                ).astype(jnp.bfloat16)
                for i in range(per):
                    d = g * per + i
                    for way in range(THIRDS):
                        top = i * rows + way * third
                        store_block(left_out, d, way, product[top:top + third])

                def send(i, carry):
                    d = g * per + (r + i) % per

                    @pl.when(d != r)
                    def _():
                        for way in range(THIRDS):
                            left_copy(d, way).start()

                    return carry

                lax.fori_loop(0, per, send, 0)
                return carry

            lax.fori_loop(0, LEFT_GROUPS, left_part, 0)
            left_in[r] = left_out[r]

        mean_copy().wait_recv()
        left[rows:, :] = jnp.broadcast_to(mean_next[...], (PAD, size)).astype(jnp.bfloat16)

        def await_left(i, carry):
            for way in range(THIRDS):
                left_arrival(ring_row((place + i) % n, n), way).wait_recv()
            return carry

        lax.fori_loop(1, n, await_left, 0)
        for d in range(n):
            for way in range(THIRDS):
                place_block(d, way)

        offsets[0] = whole_offset

        def right_part(j, carry):
            columns = pl.ds(aligned(j * part, part), part)
            product = lax.dot_general(
                left[...], gain[pl.ds(j * (n // GROUPS), n // GROUPS)].reshape(part, size),
                CONTRACT_LAST, preferred_element_type=jnp.float32,
            )
            cov_out[:, columns] = (
                product[:rows] + cov_in[:, columns].astype(jnp.float32)
            ).astype(jnp.bfloat16)
            mean = product[rows:rows + 1] + offsets[0, :, columns]
            mean_send[:, columns] = mean.astype(jnp.bfloat16).astype(jnp.float32)

            @pl.when(t > 0)
            def _():
                cov_copy(cov_out, j).start()

            store_cov(j).start()
            return carry

        lax.fori_loop(0, GROUPS, right_part, 0)
        mean_out[...] = mean_send[...]

        @pl.when(t > 0)
        def _():
            mean_copy().start()

        for j in range(GROUPS):
            store_cov(j).wait()

        def left_gone(i, carry):
            for way in range(THIRDS):
                left_copy(ring_row((place + i) % n, n), way).wait_send()
            return carry

        lax.fori_loop(1, n, left_gone, 0)

    @pl.when(t > 0)
    def _():
        for j in range(GROUPS):
            cov_copy(cov_out, j).wait_send()
        mean_copy().wait_send()

    def offset_gone(i, carry):
        offset_copy(i).wait_send()
        return carry

    lax.fori_loop(1, n, offset_gone, 0)


def shards(steps, n, smoother_gains, smoother_offsets, smoother_covs):
    own_gain = smoother_gains[0]
    own_cov = smoother_covs[0]
    rows, size = own_cov.shape
    start = lax.axis_index("rows") * rows
    offset_row = lax.dynamic_update_slice(
        jnp.zeros((1, size), jnp.float32), smoother_offsets.astype(jnp.float32), (0, start)
    )
    vmem = pl.BlockSpec(memory_space=pltpu.VMEM)
    hbm = pl.BlockSpec(memory_space=pl.ANY)
    lanes = main_lanes(rows)
    folded = (n, THIRDS, rows // THIRDS * rows // lanes, lanes)
    dma = pltpu.SemaphoreType.DMA
    mean_row, cov = pl.pallas_call(
        functools.partial(kernel, steps, n),
        out_shape=(
            jax.ShapeDtypeStruct((1, size), jnp.float32),
            jax.ShapeDtypeStruct((rows, size), jnp.bfloat16),
        ),
        in_specs=[hbm, vmem, hbm],
        out_specs=(vmem, hbm),
        scratch_shapes=[
            pltpu.VMEM((n, rows, size), jnp.bfloat16),
            pltpu.VMEM((rows, size), jnp.bfloat16),
            pltpu.VMEM((rows, size), jnp.bfloat16),
            pltpu.VMEM((rows, size), jnp.bfloat16),
            pltpu.VMEM(folded, jnp.bfloat16),
            pltpu.VMEM(folded, jnp.bfloat16),
            pltpu.VMEM((rows + PAD, size), jnp.bfloat16),
            pltpu.VMEM((n, 1, size), jnp.float32),
            pltpu.VMEM((1, size), jnp.float32),
            pltpu.VMEM((1, size), jnp.float32),
            dma,
            dma((2, n, PIECES // 2)),
            dma((2, n, PIECES // 2)),
            dma((THIRDS, n)),
            dma((THIRDS, n)),
            dma((n,)),
            dma((n,)),
            dma((GROUPS,)),
            dma((GROUPS,)),
            dma((2,)),
            dma,
            dma((GROUPS,)),
            pltpu.VMEM((n, 2, rows // PIECES, size), jnp.bfloat16),
            dma((2,)),
            dma((2,)),
            dma((2, n)),
            dma((2, n)),
            dma((2, n)),
            dma((2, n)),
            pltpu.SemaphoreType.REGULAR,
        ],
        compiler_params=pltpu.CompilerParams(
            collective_id=0, has_side_effects=True, vmem_limit_bytes=62 << 20
        ),
    )(own_gain, offset_row, own_cov)
    mean = lax.dynamic_slice(mean_row, (0, start), (1, rows)).astype(jnp.bfloat16)
    return mean, cov[None]


def solution(mesh):
    in_specs = (P("tm", "rows", None), P("tm", "rows"), P("tm", "rows", None))
    out_specs = (P("tm", "rows"), P("tm", "rows", None))
    body = functools.partial(shards, mesh.shape["tm"], mesh.shape["rows"])
    return jax.shard_map(body, mesh=mesh, in_specs=in_specs, out_specs=out_specs, check_vma=False)
```

```python
import functools

import jax
import jax.numpy as jnp
from jax import lax
from jax.experimental import pallas as pl
from jax.experimental.pallas import tpu as pltpu
from jax.sharding import PartitionSpec as P

MESH = pl.DeviceIdType.MESH
PIECE = 16
GROUPS = 4
LEFT_GROUPS = 2
HEAD_START = 2
PAD = 16
CONTRACT_LAST = (((1,), (1,)), ((), ()))


def ring_row(place, n):
    side = place // (n // 2)
    return (1 - side) * 2 * place + side * (2 * (n - 1 - place) + 1)


def ring_place(row, n):
    odd = row % 2
    return (1 - odd) * (row // 2) + odd * (n - 1 - row // 2)


def main_lanes(rows):
    return 128 if rows == 192 else rows


def kernel(
    steps, n, gain_in, offset_in, cov_hbm, mean_out, cov_out,
    gain, cov_in, cov_next, left_out, left_in, left, offsets, mean_next, mean_send,
    gain_sem, ring_send, ring_recv, left_send, left_recv,
    offset_send, offset_recv, cov_send, cov_recv, mean_sems, cov_sem, gate,
):
    t = lax.axis_index("tm")
    r = lax.axis_index("rows")
    place = ring_place(r, n)
    rows, size = cov_in.shape
    half = rows // 2
    piece = PIECE
    chunks = half // PIECE
    part = size // GROUPS
    left_part_rows = size // LEFT_GROUPS
    per = n // LEFT_GROUPS
    last = steps - 1
    right = ring_row((place + 1) % n, n)
    back = ring_row((place + n - 1) % n, n)

    def aligned(x, m):
        return pl.multiple_of(x, m)

    own_gain = pltpu.make_async_copy(
        gain_in, gain.at[pl.ds(aligned(r * rows, rows), rows), :], gain_sem
    )
    own_gain.start()
    own_cov = pltpu.make_async_copy(cov_hbm, cov_in, cov_sem)
    own_cov.start()

    def store_block(ref, index, way, block):
        main = main_lanes(rows)
        ref[index, way, 0:half, :] = block[:, :main]
        if main < rows:
            for i in range(2):
                ref[index, way, half:, i * 64:(i + 1) * 64] = block[
                    i * half // 2:(i + 1) * half // 2, main:
                ]

    def place_block(d, way):
        main = main_lanes(rows)
        top, at = way * half, d * rows
        left[top:top + half, at:at + main] = left_in[d, way, 0:half, :]
        if main < rows:
            for i in range(2):
                left[top + i * half // 2:top + (i + 1) * half // 2, at + main:at + rows] = (
                    left_in[d, way, half:, i * 64:(i + 1) * 64]
                )

    barrier = pltpu.get_barrier_semaphore()

    def greet(i, carry):
        other = ring_row((place + i) % n, n)
        pl.semaphore_signal(barrier, inc=1, device_id=(t, other), device_id_type=MESH)
        return carry

    lax.fori_loop(1, n, greet, 0)

    @pl.when(t > 0)
    def _():
        pl.semaphore_signal(barrier, inc=1, device_id=(t - 1, r), device_id_type=MESH)

    @pl.when(t < last)
    def _():
        pl.semaphore_signal(barrier, inc=1, device_id=(t + 1, r), device_id_type=MESH)

    pl.semaphore_wait(barrier, n - 1 + (t + last - 1) // last + (2 * last - t - 1) // last)

    def cov_copy(source, j):
        columns = pl.ds(aligned(j * part, part), part)
        return pltpu.make_async_remote_copy(
            src_ref=source.at[:, columns],
            dst_ref=cov_next.at[:, columns],
            send_sem=cov_send.at[j],
            recv_sem=cov_recv.at[j],
            device_id=(t - 1, r),
            device_id_type=MESH,
        )

    def mean_copy():
        return pltpu.make_async_remote_copy(
            src_ref=mean_send,
            dst_ref=mean_next,
            send_sem=mean_sems.at[0],
            recv_sem=mean_sems.at[1],
            device_id=(t - 1, r),
            device_id_type=MESH,
        )

    def offset_copy(i):
        other = ring_row((place + i) % n, n)
        return pltpu.make_async_remote_copy(
            src_ref=offset_in,
            dst_ref=offsets.at[r],
            send_sem=offset_send.at[i],
            recv_sem=offset_recv.at[r],
            device_id=(t, other),
            device_id_type=MESH,
        )

    def offset_arrival(i):
        other = ring_row((place + i) % n, n)
        return pltpu.make_async_remote_copy(
            src_ref=offset_in,
            dst_ref=offsets.at[other],
            send_sem=offset_send.at[i],
            recv_sem=offset_recv.at[other],
            device_id=(t, other),
            device_id_type=MESH,
        )

    def ring_copy(way, hop, c):
        origin = ring_row((place + (n - hop if way == 0 else hop)) % n, n)
        span = pl.ds(aligned(origin * rows + way * half + c * piece, piece), piece)
        return pltpu.make_async_remote_copy(
            src_ref=gain.at[span, :],
            dst_ref=gain.at[span, :],
            send_sem=ring_send.at[way, hop, c],
            recv_sem=ring_recv.at[way, hop, c],
            device_id=(t, right if way == 0 else back),
            device_id_type=MESH,
        )

    def ring_arrival(way, hop, c):
        origin = ring_row((place + (n - 1 - hop if way == 0 else hop + 1)) % n, n)
        span = pl.ds(aligned(origin * rows + way * half + c * piece, piece), piece)
        return pltpu.make_async_remote_copy(
            src_ref=gain.at[span, :],
            dst_ref=gain.at[span, :],
            send_sem=ring_send.at[way, hop, c],
            recv_sem=ring_recv.at[way, hop, c],
            device_id=(t, right if way == 0 else back),
            device_id_type=MESH,
        )

    def left_copy(d, way):
        return pltpu.make_async_remote_copy(
            src_ref=left_out.at[d, way],
            dst_ref=left_in.at[r, way],
            send_sem=left_send.at[way, d],
            recv_sem=left_recv.at[way, r],
            device_id=(t, d),
            device_id_type=MESH,
        )

    def left_arrival(d, way):
        return pltpu.make_async_remote_copy(
            src_ref=left_out.at[d, way],
            dst_ref=left_in.at[d, way],
            send_sem=left_send.at[way, d],
            recv_sem=left_recv.at[way, d],
            device_id=(t, d),
            device_id_type=MESH,
        )

    def await_cov():
        for j in range(GROUPS):
            cov_copy(cov_in, j).wait_recv()

    own_cov.wait()

    @pl.when(t == last)
    def _():
        for j in range(GROUPS):
            cov_copy(cov_in, j).start()

    def send_offset(i, carry):
        offset_copy(i).start()
        return carry

    lax.fori_loop(1, n, send_offset, 0)
    own_gain.wait()

    def left_half(d, way):
        block = gain[pl.ds(aligned(d * rows + way * half, half), half), :]
        product = lax.dot_general(
            block, cov_next[...], CONTRACT_LAST, preferred_element_type=jnp.float32
        )
        return product.astype(jnp.bfloat16)

    @pl.when(t < last)
    def _():
        @pl.when(t % 2 == 0)
        def _():
            @pl.when(t < last - 1)
            def _():
                pl.semaphore_wait(gate, 1)

        for c in range(chunks):
            for way in range(2):
                ring_copy(way, 0, c).start()

        @pl.when(t == last - 1)
        def _():
            await_cov()
            for way in range(2):
                store_block(left_in, r, way, left_half(r, way))

        def pass_on(hop, carry):
            for c in range(chunks):
                for way in range(2):
                    ring_arrival(way, hop - 1, c).wait_recv()
                    ring_copy(way, hop, c).start()

            @pl.when(hop == min(HEAD_START, n - 2))
            def _():
                @pl.when(t % 2 == 1)
                def _():
                    pl.semaphore_signal(gate, inc=1, device_id=(t - 1, r), device_id_type=MESH)

            @pl.when(t == last - 1)
            def _():
                for way in range(2):
                    d = ring_row((place + (n - hop if way == 0 else hop)) % n, n)
                    store_block(left_out, d, way, left_half(d, way))
                    left_copy(d, way).start()

            return carry

        lax.fori_loop(1, n - 1, pass_on, 0)

        for c in range(chunks):
            for way in range(2):
                ring_arrival(way, n - 2, c).wait_recv()

        @pl.when(t == last - 1)
        def _():
            for way in range(2):
                d = ring_row((place + (1 if way == 0 else n - 1)) % n, n)
                store_block(left_out, d, way, left_half(d, way))
                left_copy(d, way).start()

    offsets[r] = offset_in[...]

    def await_offset(i, carry):
        offset_arrival(i).wait_recv()
        return carry

    lax.fori_loop(1, n, await_offset, 0)
    whole_offset = offsets[0]
    for i in range(1, n):
        whole_offset = whole_offset + offsets[i]

    @pl.when(t == last)
    def _():
        mean_send[...] = whole_offset
        mean_copy().start()
        mean_out[...] = whole_offset
        cov_out[...] = cov_in[...]

    @pl.when(t < last)
    def _():
        @pl.when(t < last - 1)
        def _():
            await_cov()

            def left_part(j, carry):
                g = (r // per + 1 + j) % LEFT_GROUPS
                span = pl.ds(aligned(g * left_part_rows, left_part_rows), left_part_rows)
                product = lax.dot_general(
                    gain[span, :], cov_next[...], CONTRACT_LAST,
                    preferred_element_type=jnp.float32,
                ).astype(jnp.bfloat16)
                for i in range(per):
                    d = g * per + i
                    for way in range(2):
                        top = i * rows + way * half
                        store_block(left_out, d, way, product[top:top + half])

                def send(i, carry):
                    d = g * per + (r + i) % per

                    @pl.when(d != r)
                    def _():
                        for way in range(2):
                            left_copy(d, way).start()

                    return carry

                lax.fori_loop(0, per, send, 0)
                return carry

            lax.fori_loop(0, LEFT_GROUPS, left_part, 0)
            left_in[r] = left_out[r]

        mean_copy().wait_recv()
        left[rows:, :] = jnp.broadcast_to(mean_next[...], (PAD, size)).astype(jnp.bfloat16)

        def await_left(i, carry):
            for way in range(2):
                left_arrival(ring_row((place + i) % n, n), way).wait_recv()
            return carry

        lax.fori_loop(1, n, await_left, 0)
        for d in range(n):
            for way in range(2):
                place_block(d, way)

        offsets[0] = whole_offset

        def right_part(j, carry):
            columns = pl.ds(aligned(j * part, part), part)
            product = lax.dot_general(
                left[...], gain[columns, :], CONTRACT_LAST, preferred_element_type=jnp.float32
            )
            cov_out[:, columns] = (
                product[:rows] + cov_in[:, columns].astype(jnp.float32)
            ).astype(jnp.bfloat16)
            mean = product[rows:rows + 1] + offsets[0, :, columns]
            mean_send[:, columns] = mean.astype(jnp.bfloat16).astype(jnp.float32)

            @pl.when(t > 0)
            def _():
                cov_copy(cov_out, j).start()

            return carry

        lax.fori_loop(0, GROUPS, right_part, 0)
        mean_out[...] = mean_send[...]

        @pl.when(t > 0)
        def _():
            mean_copy().start()

        def left_gone(i, carry):
            for way in range(2):
                left_copy(ring_row((place + i) % n, n), way).wait_send()
            return carry

        lax.fori_loop(1, n, left_gone, 0)

        def ring_gone(hop, carry):
            for c in range(chunks):
                for way in range(2):
                    ring_copy(way, hop, c).wait_send()
            return carry

        lax.fori_loop(0, n - 1, ring_gone, 0)

    @pl.when(t > 0)
    def _():
        for j in range(GROUPS):
            cov_copy(cov_out, j).wait_send()
        mean_copy().wait_send()

    def offset_gone(i, carry):
        offset_copy(i).wait_send()
        return carry

    lax.fori_loop(1, n, offset_gone, 0)


def shards(steps, n, smoother_gains, smoother_offsets, smoother_covs):
    own_gain = smoother_gains[0]
    own_cov = smoother_covs[0]
    rows, size = own_cov.shape
    start = lax.axis_index("rows") * rows
    offset_row = lax.dynamic_update_slice(
        jnp.zeros((1, size), jnp.float32), smoother_offsets.astype(jnp.float32), (0, start)
    )
    vmem = pl.BlockSpec(memory_space=pltpu.VMEM)
    hbm = pl.BlockSpec(memory_space=pltpu.HBM)
    lanes = main_lanes(rows)
    folded = (n, 2, rows // 2 * rows // lanes, lanes)
    dma = pltpu.SemaphoreType.DMA
    mean_row, cov = pl.pallas_call(
        functools.partial(kernel, steps, n),
        out_shape=(
            jax.ShapeDtypeStruct((1, size), jnp.float32),
            jax.ShapeDtypeStruct((rows, size), jnp.bfloat16),
        ),
        in_specs=[hbm, vmem, hbm],
        out_specs=(vmem, vmem),
        scratch_shapes=[
            pltpu.VMEM((size, size), jnp.bfloat16),
            pltpu.VMEM((rows, size), jnp.bfloat16),
            pltpu.VMEM((rows, size), jnp.bfloat16),
            pltpu.VMEM(folded, jnp.bfloat16),
            pltpu.VMEM(folded, jnp.bfloat16),
            pltpu.VMEM((rows + PAD, size), jnp.bfloat16),
            pltpu.VMEM((n, 1, size), jnp.float32),
            pltpu.VMEM((1, size), jnp.float32),
            pltpu.VMEM((1, size), jnp.float32),
            dma,
            dma((2, n, rows // 2 // PIECE)),
            dma((2, n, rows // 2 // PIECE)),
            dma((2, n)),
            dma((2, n)),
            dma((n,)),
            dma((n,)),
            dma((GROUPS,)),
            dma((GROUPS,)),
            dma((2,)),
            dma,
            pltpu.SemaphoreType.REGULAR,
        ],
        compiler_params=pltpu.CompilerParams(
            collective_id=0, has_side_effects=True, vmem_limit_bytes=40 << 20
        ),
    )(pltpu.with_memory_space_constraint(own_gain, pltpu.HBM), offset_row, pltpu.with_memory_space_constraint(own_cov, pltpu.HBM))
    mean = lax.dynamic_slice(mean_row, (0, start), (1, rows)).astype(jnp.bfloat16)
    return mean, cov[None]


def solution(mesh):
    in_specs = (P("tm", "rows", None), P("tm", "rows"), P("tm", "rows", None))
    out_specs = (P("tm", "rows"), P("tm", "rows", None))
    body = functools.partial(shards, mesh.shape["tm"], mesh.shape["rows"])
    return jax.shard_map(body, mesh=mesh, in_specs=in_specs, out_specs=out_specs, check_vma=False)
```

```python
import functools

import jax
import jax.numpy as jnp
from jax import lax
from jax.experimental import pallas as pl
from jax.experimental.pallas import tpu as pltpu
from jax.sharding import PartitionSpec as P

MESH = pl.DeviceIdType.MESH
PIECE = 16
GROUPS = 4
LEFT_GROUPS = 2
HEAD_START = 2
PAD = 16
CONTRACT_LAST = (((1,), (1,)), ((), ()))


def ring_row(place, n):
    side = place // (n // 2)
    return (1 - side) * 2 * place + side * (2 * (n - 1 - place) + 1)


def ring_place(row, n):
    odd = row % 2
    return (1 - odd) * (row // 2) + odd * (n - 1 - row // 2)


def main_lanes(rows):
    return 128 if rows == 192 else rows


def kernel(
    steps, n, gain_in, offset_in, cov_hbm, mean_out, cov_out,
    gain, cov_in, cov_next, left_out, left_in, left, offsets, mean_next, mean_send,
    gain_sem, ring_send, ring_recv, left_send, left_recv,
    offset_send, offset_recv, cov_send, cov_recv, mean_sems, cov_sem, partial, gate,
):
    t = lax.axis_index("tm")
    r = lax.axis_index("rows")
    place = ring_place(r, n)
    rows, size = cov_in.shape
    half = rows // 2
    piece = PIECE
    chunks = half // PIECE
    part = size // GROUPS
    left_part_rows = size // LEFT_GROUPS
    per = n // LEFT_GROUPS
    last = steps - 1
    right = ring_row((place + 1) % n, n)
    back = ring_row((place + n - 1) % n, n)

    def aligned(x, m):
        return pl.multiple_of(x, m)

    own_gain = pltpu.make_async_copy(
        gain_in, gain.at[pl.ds(aligned(r * rows, rows), rows), :], gain_sem
    )
    own_gain.start()
    own_cov = pltpu.make_async_copy(cov_hbm, cov_in, cov_sem)
    own_cov.start()

    def store_block(ref, index, way, block):
        main = main_lanes(rows)
        ref[index, way, 0:half, :] = block[:, :main]
        if main < rows:
            for i in range(2):
                ref[index, way, half:, i * 64:(i + 1) * 64] = block[
                    i * half // 2:(i + 1) * half // 2, main:
                ]

    def place_block(d, way):
        main = main_lanes(rows)
        top, at = way * half, d * rows
        left[top:top + half, at:at + main] = left_in[d, way, 0:half, :]
        if main < rows:
            for i in range(2):
                left[top + i * half // 2:top + (i + 1) * half // 2, at + main:at + rows] = (
                    left_in[d, way, half:, i * 64:(i + 1) * 64]
                )

    barrier = pltpu.get_barrier_semaphore()

    def greet(i, carry):
        other = ring_row((place + i) % n, n)
        pl.semaphore_signal(barrier, inc=1, device_id=(t, other), device_id_type=MESH)
        return carry

    lax.fori_loop(1, n, greet, 0)

    @pl.when(t > 0)
    def _():
        pl.semaphore_signal(barrier, inc=1, device_id=(t - 1, r), device_id_type=MESH)

    @pl.when(t < last)
    def _():
        pl.semaphore_signal(barrier, inc=1, device_id=(t + 1, r), device_id_type=MESH)

    pl.semaphore_wait(barrier, n - 1 + (t + last - 1) // last + (2 * last - t - 1) // last)

    def cov_copy(source, j):
        columns = pl.ds(aligned(j * part, part), part)
        return pltpu.make_async_remote_copy(
            src_ref=source.at[:, columns],
            dst_ref=cov_next.at[:, columns],
            send_sem=cov_send.at[j],
            recv_sem=cov_recv.at[j],
            device_id=(t - 1, r),
            device_id_type=MESH,
        )

    def mean_copy():
        return pltpu.make_async_remote_copy(
            src_ref=mean_send,
            dst_ref=mean_next,
            send_sem=mean_sems.at[0],
            recv_sem=mean_sems.at[1],
            device_id=(t - 1, r),
            device_id_type=MESH,
        )

    def offset_copy(i):
        other = ring_row((place + i) % n, n)
        return pltpu.make_async_remote_copy(
            src_ref=offset_in,
            dst_ref=offsets.at[r],
            send_sem=offset_send.at[i],
            recv_sem=offset_recv.at[r],
            device_id=(t, other),
            device_id_type=MESH,
        )

    def offset_arrival(i):
        other = ring_row((place + i) % n, n)
        return pltpu.make_async_remote_copy(
            src_ref=offset_in,
            dst_ref=offsets.at[other],
            send_sem=offset_send.at[i],
            recv_sem=offset_recv.at[other],
            device_id=(t, other),
            device_id_type=MESH,
        )

    def ring_copy(way, hop, c):
        origin = ring_row((place + (n - hop if way == 0 else hop)) % n, n)
        span = pl.ds(aligned(origin * rows + way * half + c * piece, piece), piece)
        return pltpu.make_async_remote_copy(
            src_ref=gain.at[span, :],
            dst_ref=gain.at[span, :],
            send_sem=ring_send.at[way, hop, c],
            recv_sem=ring_recv.at[way, hop, c],
            device_id=(t, right if way == 0 else back),
            device_id_type=MESH,
        )

    def ring_arrival(way, hop, c):
        origin = ring_row((place + (n - 1 - hop if way == 0 else hop + 1)) % n, n)
        span = pl.ds(aligned(origin * rows + way * half + c * piece, piece), piece)
        return pltpu.make_async_remote_copy(
            src_ref=gain.at[span, :],
            dst_ref=gain.at[span, :],
            send_sem=ring_send.at[way, hop, c],
            recv_sem=ring_recv.at[way, hop, c],
            device_id=(t, right if way == 0 else back),
            device_id_type=MESH,
        )

    def left_copy(d, way):
        return pltpu.make_async_remote_copy(
            src_ref=left_out.at[d, way],
            dst_ref=left_in.at[r, way],
            send_sem=left_send.at[way, d],
            recv_sem=left_recv.at[way, r],
            device_id=(t, d),
            device_id_type=MESH,
        )

    def left_arrival(d, way):
        return pltpu.make_async_remote_copy(
            src_ref=left_out.at[d, way],
            dst_ref=left_in.at[d, way],
            send_sem=left_send.at[way, d],
            recv_sem=left_recv.at[way, d],
            device_id=(t, d),
            device_id_type=MESH,
        )

    def await_cov():
        for j in range(GROUPS):
            cov_copy(cov_in, j).wait_recv()

    own_cov.wait()

    @pl.when(t == last)
    def _():
        for j in range(GROUPS):
            cov_copy(cov_in, j).start()

    def send_offset(i, carry):
        offset_copy(i).start()
        return carry

    lax.fori_loop(1, n, send_offset, 0)
    own_gain.wait()

    def left_half(d, way):
        block = gain[pl.ds(aligned(d * rows + way * half, half), half), :]
        product = lax.dot_general(
            block, cov_next[...], CONTRACT_LAST, preferred_element_type=jnp.float32
        )
        return product.astype(jnp.bfloat16)

    @pl.when(t < last)
    def _():
        @pl.when(t % 2 == 0)
        def _():
            @pl.when(t < last - 1)
            def _():
                pl.semaphore_wait(gate, 1)

        for c in range(chunks):
            for way in range(2):
                ring_copy(way, 0, c).start()

        @pl.when(t == last - 1)
        def _():
            await_cov()
            for way in range(2):
                store_block(left_in, r, way, left_half(r, way))

        def pass_on(hop, carry):
            for c in range(chunks):
                for way in range(2):
                    ring_arrival(way, hop - 1, c).wait_recv()
                    ring_copy(way, hop, c).start()

            @pl.when(hop == min(HEAD_START, n - 2))
            def _():
                @pl.when(t % 2 == 1)
                def _():
                    pl.semaphore_signal(gate, inc=1, device_id=(t - 1, r), device_id_type=MESH)

            @pl.when(t == last - 1)
            def _():
                for way in range(2):
                    d = ring_row((place + (n - hop if way == 0 else hop)) % n, n)
                    store_block(left_out, d, way, left_half(d, way))
                    left_copy(d, way).start()

            return carry

        lax.fori_loop(1, n - 1, pass_on, 0)

        for c in range(chunks):
            for way in range(2):
                ring_arrival(way, n - 2, c).wait_recv()

        @pl.when(t == last - 1)
        def _():
            for way in range(2):
                d = ring_row((place + (1 if way == 0 else n - 1)) % n, n)
                store_block(left_out, d, way, left_half(d, way))
                left_copy(d, way).start()

    offsets[r] = offset_in[...]

    def await_offset(i, carry):
        offset_arrival(i).wait_recv()
        return carry

    lax.fori_loop(1, n, await_offset, 0)
    whole_offset = offsets[0]
    for i in range(1, n):
        whole_offset = whole_offset + offsets[i]

    @pl.when(t == last)
    def _():
        mean_send[...] = whole_offset
        mean_copy().start()
        mean_out[...] = whole_offset
        cov_out[...] = cov_in[...]

    @pl.when(t < last)
    def _():
        @pl.when(t < last - 1)
        def _():
            await_cov()

            def left_part(j, carry):
                g = (r // per + 1 + j) % LEFT_GROUPS
                span = pl.ds(aligned(g * left_part_rows, left_part_rows), left_part_rows)
                product = lax.dot_general(
                    gain[span, :], cov_next[...], CONTRACT_LAST,
                    preferred_element_type=jnp.float32,
                ).astype(jnp.bfloat16)
                for i in range(per):
                    d = g * per + i
                    for way in range(2):
                        top = i * rows + way * half
                        store_block(left_out, d, way, product[top:top + half])

                def send(i, carry):
                    d = g * per + (r + i) % per

                    @pl.when(d != r)
                    def _():
                        for way in range(2):
                            left_copy(d, way).start()

                    return carry

                lax.fori_loop(0, per, send, 0)
                return carry

            lax.fori_loop(0, LEFT_GROUPS, left_part, 0)
            left_in[r] = left_out[r]

        mean_copy().wait_recv()
        left[rows:, :] = jnp.broadcast_to(mean_next[...], (PAD, size)).astype(jnp.bfloat16)

        near = r // per

        def gather_half(h):
            for i in range(per):
                d = h * per + i

                @pl.when(d != r)
                def _():
                    for way in range(2):
                        left_arrival(d, way).wait_recv()

            for g in range(LEFT_GROUPS):
                @pl.when(h == g)
                def _():
                    for i in range(per):
                        for way in range(2):
                            place_block(g * per + i, way)

            return pl.ds(aligned(h * left_part_rows, left_part_rows), left_part_rows)

        near_inner = gather_half(near)

        def near_part(j, carry):
            columns = pl.ds(aligned(j * left_part_rows, left_part_rows), left_part_rows)
            partial[:, columns] = lax.dot_general(
                left[:, near_inner], gain[columns, near_inner], CONTRACT_LAST,
                preferred_element_type=jnp.float32,
            )
            return carry

        lax.fori_loop(0, LEFT_GROUPS, near_part, 0)
        far_inner = gather_half(1 - near)
        offsets[0] = whole_offset

        def right_part(j, carry):
            columns = pl.ds(aligned(j * part, part), part)
            product = partial[:, columns] + lax.dot_general(
                left[:, far_inner], gain[columns, far_inner], CONTRACT_LAST,
                preferred_element_type=jnp.float32,
            )
            cov_out[:, columns] = (
                product[:rows] + cov_in[:, columns].astype(jnp.float32)
            ).astype(jnp.bfloat16)
            mean = product[rows:rows + 1] + offsets[0, :, columns]
            mean_send[:, columns] = mean.astype(jnp.bfloat16).astype(jnp.float32)

            @pl.when(t > 0)
            def _():
                cov_copy(cov_out, j).start()

            return carry

        lax.fori_loop(0, GROUPS, right_part, 0)
        mean_out[...] = mean_send[...]

        @pl.when(t > 0)
        def _():
            mean_copy().start()

        def left_gone(i, carry):
            for way in range(2):
                left_copy(ring_row((place + i) % n, n), way).wait_send()
            return carry

        lax.fori_loop(1, n, left_gone, 0)

        def ring_gone(hop, carry):
            for c in range(chunks):
                for way in range(2):
                    ring_copy(way, hop, c).wait_send()
            return carry

        lax.fori_loop(0, n - 1, ring_gone, 0)

    @pl.when(t > 0)
    def _():
        for j in range(GROUPS):
            cov_copy(cov_out, j).wait_send()
        mean_copy().wait_send()

    def offset_gone(i, carry):
        offset_copy(i).wait_send()
        return carry

    lax.fori_loop(1, n, offset_gone, 0)


def shards(steps, n, smoother_gains, smoother_offsets, smoother_covs):
    own_gain = smoother_gains[0]
    own_cov = smoother_covs[0]
    rows, size = own_cov.shape
    start = lax.axis_index("rows") * rows
    offset_row = lax.dynamic_update_slice(
        jnp.zeros((1, size), jnp.float32), smoother_offsets.astype(jnp.float32), (0, start)
    )
    vmem = pl.BlockSpec(memory_space=pltpu.VMEM)
    hbm = pl.BlockSpec(memory_space=pltpu.HBM)
    lanes = main_lanes(rows)
    folded = (n, 2, rows // 2 * rows // lanes, lanes)
    dma = pltpu.SemaphoreType.DMA
    mean_row, cov = pl.pallas_call(
        functools.partial(kernel, steps, n),
        out_shape=(
            jax.ShapeDtypeStruct((1, size), jnp.float32),
            jax.ShapeDtypeStruct((rows, size), jnp.bfloat16),
        ),
        in_specs=[hbm, vmem, hbm],
        out_specs=(vmem, vmem),
        scratch_shapes=[
            pltpu.VMEM((size, size), jnp.bfloat16),
            pltpu.VMEM((rows, size), jnp.bfloat16),
            pltpu.VMEM((rows, size), jnp.bfloat16),
            pltpu.VMEM(folded, jnp.bfloat16),
            pltpu.VMEM(folded, jnp.bfloat16),
            pltpu.VMEM((rows + PAD, size), jnp.bfloat16),
            pltpu.VMEM((n, 1, size), jnp.float32),
            pltpu.VMEM((1, size), jnp.float32),
            pltpu.VMEM((1, size), jnp.float32),
            dma,
            dma((2, n, rows // 2 // PIECE)),
            dma((2, n, rows // 2 // PIECE)),
            dma((2, n)),
            dma((2, n)),
            dma((n,)),
            dma((n,)),
            dma((GROUPS,)),
            dma((GROUPS,)),
            dma((2,)),
            dma,
            pltpu.VMEM((rows + PAD, size), jnp.float32),
            pltpu.SemaphoreType.REGULAR,
        ],
        compiler_params=pltpu.CompilerParams(
            collective_id=0, has_side_effects=True, vmem_limit_bytes=40 << 20
        ),
    )(pltpu.with_memory_space_constraint(own_gain, pltpu.HBM), offset_row, pltpu.with_memory_space_constraint(own_cov, pltpu.HBM))
    mean = lax.dynamic_slice(mean_row, (0, start), (1, rows)).astype(jnp.bfloat16)
    return mean, cov[None]


def solution(mesh):
    in_specs = (P("tm", "rows", None), P("tm", "rows"), P("tm", "rows", None))
    out_specs = (P("tm", "rows"), P("tm", "rows", None))
    body = functools.partial(shards, mesh.shape["tm"], mesh.shape["rows"])
    return jax.shard_map(body, mesh=mesh, in_specs=in_specs, out_specs=out_specs, check_vma=False)
```

```python
import functools

import jax
import jax.numpy as jnp
from jax import lax
from jax.experimental import pallas as pl
from jax.experimental.pallas import tpu as pltpu
from jax.sharding import PartitionSpec as P

MESH = pl.DeviceIdType.MESH
PIECE = 16
GROUPS = 4
LEFT_GROUPS = 2
HEAD_START = 1
PAD = 16
CONTRACT_LAST = (((1,), (1,)), ((), ()))


def ring_row(place, n):
    side = place // (n // 2)
    return (1 - side) * 2 * place + side * (2 * (n - 1 - place) + 1)


def ring_place(row, n):
    odd = row % 2
    return (1 - odd) * (row // 2) + odd * (n - 1 - row // 2)


def main_lanes(rows):
    return 128 if rows == 192 else rows


def kernel(
    steps, n, gain_in, offset_in, cov_hbm, mean_out, cov_out,
    gain, cov_in, cov_next, left_out, left_in, left, offsets, mean_next, mean_send,
    gain_sem, ring_send, ring_recv, left_send, left_recv,
    offset_send, offset_recv, cov_send, cov_recv, mean_sems, cov_sem, partial, gate,
):
    t = lax.axis_index("tm")
    r = lax.axis_index("rows")
    place = ring_place(r, n)
    rows, size = cov_in.shape
    half = rows // 2
    piece = PIECE
    chunks = half // PIECE
    part = size // GROUPS
    left_part_rows = size // LEFT_GROUPS
    per = n // LEFT_GROUPS
    last = steps - 1
    right = ring_row((place + 1) % n, n)
    back = ring_row((place + n - 1) % n, n)

    def aligned(x, m):
        return pl.multiple_of(x, m)

    own_gain = pltpu.make_async_copy(
        gain_in, gain.at[pl.ds(aligned(r * rows, rows), rows), :], gain_sem
    )
    own_gain.start()
    own_cov = pltpu.make_async_copy(cov_hbm, cov_in, cov_sem)
    own_cov.start()

    def store_block(ref, index, way, block):
        main = main_lanes(rows)
        ref[index, way, 0:half, :] = block[:, :main]
        if main < rows:
            for i in range(2):
                ref[index, way, half:, i * 64:(i + 1) * 64] = block[
                    i * half // 2:(i + 1) * half // 2, main:
                ]

    def place_block(d, way):
        main = main_lanes(rows)
        top, at = way * half, d * rows
        left[top:top + half, at:at + main] = left_in[d, way, 0:half, :]
        if main < rows:
            for i in range(2):
                left[top + i * half // 2:top + (i + 1) * half // 2, at + main:at + rows] = (
                    left_in[d, way, half:, i * 64:(i + 1) * 64]
                )

    barrier = pltpu.get_barrier_semaphore()

    def greet(i, carry):
        other = ring_row((place + i) % n, n)
        pl.semaphore_signal(barrier, inc=1, device_id=(t, other), device_id_type=MESH)
        return carry

    lax.fori_loop(1, n, greet, 0)

    @pl.when(t > 0)
    def _():
        pl.semaphore_signal(barrier, inc=1, device_id=(t - 1, r), device_id_type=MESH)

    @pl.when(t < last)
    def _():
        pl.semaphore_signal(barrier, inc=1, device_id=(t + 1, r), device_id_type=MESH)

    pl.semaphore_wait(barrier, n - 1 + (t + last - 1) // last + (2 * last - t - 1) // last)

    def cov_copy(source, j):
        columns = pl.ds(aligned(j * part, part), part)
        return pltpu.make_async_remote_copy(
            src_ref=source.at[:, columns],
            dst_ref=cov_next.at[:, columns],
            send_sem=cov_send.at[j],
            recv_sem=cov_recv.at[j],
            device_id=(t - 1, r),
            device_id_type=MESH,
        )

    def mean_copy():
        return pltpu.make_async_remote_copy(
            src_ref=mean_send,
            dst_ref=mean_next,
            send_sem=mean_sems.at[0],
            recv_sem=mean_sems.at[1],
            device_id=(t - 1, r),
            device_id_type=MESH,
        )

    def offset_copy(i):
        other = ring_row((place + i) % n, n)
        return pltpu.make_async_remote_copy(
            src_ref=offset_in,
            dst_ref=offsets.at[r],
            send_sem=offset_send.at[i],
            recv_sem=offset_recv.at[r],
            device_id=(t, other),
            device_id_type=MESH,
        )

    def offset_arrival(i):
        other = ring_row((place + i) % n, n)
        return pltpu.make_async_remote_copy(
            src_ref=offset_in,
            dst_ref=offsets.at[other],
            send_sem=offset_send.at[i],
            recv_sem=offset_recv.at[other],
            device_id=(t, other),
            device_id_type=MESH,
        )

    def ring_copy(way, hop, c):
        origin = ring_row((place + (n - hop if way == 0 else hop)) % n, n)
        span = pl.ds(aligned(origin * rows + way * half + c * piece, piece), piece)
        return pltpu.make_async_remote_copy(
            src_ref=gain.at[span, :],
            dst_ref=gain.at[span, :],
            send_sem=ring_send.at[way, hop, c],
            recv_sem=ring_recv.at[way, hop, c],
            device_id=(t, right if way == 0 else back),
            device_id_type=MESH,
        )

    def ring_arrival(way, hop, c):
        origin = ring_row((place + (n - 1 - hop if way == 0 else hop + 1)) % n, n)
        span = pl.ds(aligned(origin * rows + way * half + c * piece, piece), piece)
        return pltpu.make_async_remote_copy(
            src_ref=gain.at[span, :],
            dst_ref=gain.at[span, :],
            send_sem=ring_send.at[way, hop, c],
            recv_sem=ring_recv.at[way, hop, c],
            device_id=(t, right if way == 0 else back),
            device_id_type=MESH,
        )

    def left_copy(d, way):
        return pltpu.make_async_remote_copy(
            src_ref=left_out.at[d, way],
            dst_ref=left_in.at[r, way],
            send_sem=left_send.at[way, d],
            recv_sem=left_recv.at[way, r],
            device_id=(t, d),
            device_id_type=MESH,
        )

    def left_arrival(d, way):
        return pltpu.make_async_remote_copy(
            src_ref=left_out.at[d, way],
            dst_ref=left_in.at[d, way],
            send_sem=left_send.at[way, d],
            recv_sem=left_recv.at[way, d],
            device_id=(t, d),
            device_id_type=MESH,
        )

    def await_cov():
        for j in range(GROUPS):
            cov_copy(cov_in, j).wait_recv()

    own_cov.wait()

    @pl.when(t == last)
    def _():
        for j in range(GROUPS):
            cov_copy(cov_in, j).start()

    def send_offset(i, carry):
        offset_copy(i).start()
        return carry

    lax.fori_loop(1, n, send_offset, 0)
    own_gain.wait()

    def left_half(d, way):
        block = gain[pl.ds(aligned(d * rows + way * half, half), half), :]
        product = lax.dot_general(
            block, cov_next[...], CONTRACT_LAST, preferred_element_type=jnp.float32
        )
        return product.astype(jnp.bfloat16)

    @pl.when(t < last)
    def _():
        @pl.when(t % 2 == 0)
        def _():
            @pl.when(t < last - 1)
            def _():
                pl.semaphore_wait(gate, 1)

        for c in range(chunks):
            for way in range(2):
                ring_copy(way, 0, c).start()

        @pl.when(t == last - 1)
        def _():
            await_cov()
            for way in range(2):
                store_block(left_in, r, way, left_half(r, way))

        def pass_on(hop, carry):
            for c in range(chunks):
                for way in range(2):
                    ring_arrival(way, hop - 1, c).wait_recv()
                    ring_copy(way, hop, c).start()

            @pl.when(hop == min(HEAD_START, n - 2))
            def _():
                @pl.when(t % 2 == 1)
                def _():
                    pl.semaphore_signal(gate, inc=1, device_id=(t - 1, r), device_id_type=MESH)

            @pl.when(t == last - 1)
            def _():
                for way in range(2):
                    d = ring_row((place + (n - hop if way == 0 else hop)) % n, n)
                    store_block(left_out, d, way, left_half(d, way))
                    left_copy(d, way).start()

            return carry

        lax.fori_loop(1, n - 1, pass_on, 0)

        for c in range(chunks):
            for way in range(2):
                ring_arrival(way, n - 2, c).wait_recv()

        @pl.when(t == last - 1)
        def _():
            for way in range(2):
                d = ring_row((place + (1 if way == 0 else n - 1)) % n, n)
                store_block(left_out, d, way, left_half(d, way))
                left_copy(d, way).start()

    offsets[r] = offset_in[...]

    def await_offset(i, carry):
        offset_arrival(i).wait_recv()
        return carry

    lax.fori_loop(1, n, await_offset, 0)
    whole_offset = offsets[0]
    for i in range(1, n):
        whole_offset = whole_offset + offsets[i]

    @pl.when(t == last)
    def _():
        mean_send[...] = whole_offset
        mean_copy().start()
        mean_out[...] = whole_offset
        cov_out[...] = cov_in[...]

    @pl.when(t < last)
    def _():
        @pl.when(t < last - 1)
        def _():
            await_cov()

            def left_part(j, carry):
                g = (r // per + 1 + j) % LEFT_GROUPS
                span = pl.ds(aligned(g * left_part_rows, left_part_rows), left_part_rows)
                product = lax.dot_general(
                    gain[span, :], cov_next[...], CONTRACT_LAST,
                    preferred_element_type=jnp.float32,
                ).astype(jnp.bfloat16)
                for i in range(per):
                    d = g * per + i
                    for way in range(2):
                        top = i * rows + way * half
                        store_block(left_out, d, way, product[top:top + half])

                def send(i, carry):
                    d = g * per + (r + i) % per

                    @pl.when(d != r)
                    def _():
                        for way in range(2):
                            left_copy(d, way).start()

                    return carry

                lax.fori_loop(0, per, send, 0)
                return carry

            lax.fori_loop(0, LEFT_GROUPS, left_part, 0)
            left_in[r] = left_out[r]

        mean_copy().wait_recv()
        left[rows:, :] = jnp.broadcast_to(mean_next[...], (PAD, size)).astype(jnp.bfloat16)

        near = r // per

        def gather_half(h):
            for i in range(per):
                d = h * per + i

                @pl.when(d != r)
                def _():
                    for way in range(2):
                        left_arrival(d, way).wait_recv()

            for g in range(LEFT_GROUPS):
                @pl.when(h == g)
                def _():
                    for i in range(per):
                        for way in range(2):
                            place_block(g * per + i, way)

            return pl.ds(aligned(h * left_part_rows, left_part_rows), left_part_rows)

        near_inner = gather_half(near)

        def near_part(j, carry):
            columns = pl.ds(aligned(j * left_part_rows, left_part_rows), left_part_rows)
            partial[:, columns] = lax.dot_general(
                left[:, near_inner], gain[columns, near_inner], CONTRACT_LAST,
                preferred_element_type=jnp.float32,
            )
            return carry

        lax.fori_loop(0, LEFT_GROUPS, near_part, 0)
        far_inner = gather_half(1 - near)
        offsets[0] = whole_offset

        def right_part(j, carry):
            columns = pl.ds(aligned(j * part, part), part)
            product = partial[:, columns] + lax.dot_general(
                left[:, far_inner], gain[columns, far_inner], CONTRACT_LAST,
                preferred_element_type=jnp.float32,
            )
            cov_out[:, columns] = (
                product[:rows] + cov_in[:, columns].astype(jnp.float32)
            ).astype(jnp.bfloat16)
            mean = product[rows:rows + 1] + offsets[0, :, columns]
            mean_send[:, columns] = mean.astype(jnp.bfloat16).astype(jnp.float32)

            @pl.when(t > 0)
            def _():
                cov_copy(cov_out, j).start()

            return carry

        lax.fori_loop(0, GROUPS, right_part, 0)
        mean_out[...] = mean_send[...]

        @pl.when(t > 0)
        def _():
            mean_copy().start()

        def left_gone(i, carry):
            for way in range(2):
                left_copy(ring_row((place + i) % n, n), way).wait_send()
            return carry

        lax.fori_loop(1, n, left_gone, 0)

        def ring_gone(hop, carry):
            for c in range(chunks):
                for way in range(2):
                    ring_copy(way, hop, c).wait_send()
            return carry

        lax.fori_loop(0, n - 1, ring_gone, 0)

    @pl.when(t > 0)
    def _():
        for j in range(GROUPS):
            cov_copy(cov_out, j).wait_send()
        mean_copy().wait_send()

    def offset_gone(i, carry):
        offset_copy(i).wait_send()
        return carry

    lax.fori_loop(1, n, offset_gone, 0)


def shards(steps, n, smoother_gains, smoother_offsets, smoother_covs):
    own_gain = smoother_gains[0]
    own_cov = smoother_covs[0]
    rows, size = own_cov.shape
    start = lax.axis_index("rows") * rows
    offset_row = lax.dynamic_update_slice(
        jnp.zeros((1, size), jnp.float32), smoother_offsets.astype(jnp.float32), (0, start)
    )
    vmem = pl.BlockSpec(memory_space=pltpu.VMEM)
    hbm = pl.BlockSpec(memory_space=pltpu.HBM)
    lanes = main_lanes(rows)
    folded = (n, 2, rows // 2 * rows // lanes, lanes)
    dma = pltpu.SemaphoreType.DMA
    mean_row, cov = pl.pallas_call(
        functools.partial(kernel, steps, n),
        out_shape=(
            jax.ShapeDtypeStruct((1, size), jnp.float32),
            jax.ShapeDtypeStruct((rows, size), jnp.bfloat16),
        ),
        in_specs=[hbm, vmem, hbm],
        out_specs=(vmem, vmem),
        scratch_shapes=[
            pltpu.VMEM((size, size), jnp.bfloat16),
            pltpu.VMEM((rows, size), jnp.bfloat16),
            pltpu.VMEM((rows, size), jnp.bfloat16),
            pltpu.VMEM(folded, jnp.bfloat16),
            pltpu.VMEM(folded, jnp.bfloat16),
            pltpu.VMEM((rows + PAD, size), jnp.bfloat16),
            pltpu.VMEM((n, 1, size), jnp.float32),
            pltpu.VMEM((1, size), jnp.float32),
            pltpu.VMEM((1, size), jnp.float32),
            dma,
            dma((2, n, rows // 2 // PIECE)),
            dma((2, n, rows // 2 // PIECE)),
            dma((2, n)),
            dma((2, n)),
            dma((n,)),
            dma((n,)),
            dma((GROUPS,)),
            dma((GROUPS,)),
            dma((2,)),
            dma,
            pltpu.VMEM((rows + PAD, size), jnp.float32),
            pltpu.SemaphoreType.REGULAR,
        ],
        compiler_params=pltpu.CompilerParams(
            collective_id=0, has_side_effects=True, vmem_limit_bytes=40 << 20
        ),
    )(pltpu.with_memory_space_constraint(own_gain, pltpu.HBM), offset_row, pltpu.with_memory_space_constraint(own_cov, pltpu.HBM))
    mean = lax.dynamic_slice(mean_row, (0, start), (1, rows)).astype(jnp.bfloat16)
    return mean, cov[None]


def solution(mesh):
    in_specs = (P("tm", "rows", None), P("tm", "rows"), P("tm", "rows", None))
    out_specs = (P("tm", "rows"), P("tm", "rows", None))
    body = functools.partial(shards, mesh.shape["tm"], mesh.shape["rows"])
    return jax.shard_map(body, mesh=mesh, in_specs=in_specs, out_specs=out_specs, check_vma=False)
```

```python
import functools

import jax
import jax.numpy as jnp
from jax import lax
from jax.experimental import pallas as pl
from jax.experimental.pallas import tpu as pltpu
from jax.sharding import PartitionSpec as P

MESH = pl.DeviceIdType.MESH
PIECE = 16
GROUPS = 3
LEFT_GROUPS = 2
HEAD_START = 2
PAD = 16
CONTRACT_LAST = (((1,), (1,)), ((), ()))


def ring_row(place, n):
    side = place // (n // 2)
    return (1 - side) * 2 * place + side * (2 * (n - 1 - place) + 1)


def ring_place(row, n):
    odd = row % 2
    return (1 - odd) * (row // 2) + odd * (n - 1 - row // 2)


def main_lanes(rows):
    return 128 if rows == 192 else rows


def kernel(
    steps, n, gain_in, offset_in, cov_hbm, mean_out, cov_out,
    gain, cov_in, cov_next, left_out, left_in, left, offsets, mean_next, mean_send,
    gain_sem, ring_send, ring_recv, left_send, left_recv,
    offset_send, offset_recv, cov_send, cov_recv, mean_sems, cov_sem, partial, gate,
):
    t = lax.axis_index("tm")
    r = lax.axis_index("rows")
    place = ring_place(r, n)
    rows, size = cov_in.shape
    half = rows // 2
    piece = PIECE
    chunks = half // PIECE
    part = size // GROUPS
    left_part_rows = size // LEFT_GROUPS
    per = n // LEFT_GROUPS
    last = steps - 1
    right = ring_row((place + 1) % n, n)
    back = ring_row((place + n - 1) % n, n)

    def aligned(x, m):
        return pl.multiple_of(x, m)

    own_gain = pltpu.make_async_copy(
        gain_in, gain.at[pl.ds(aligned(r * rows, rows), rows), :], gain_sem
    )
    own_gain.start()
    own_cov = pltpu.make_async_copy(cov_hbm, cov_in, cov_sem)
    own_cov.start()

    def store_block(ref, index, way, block):
        main = main_lanes(rows)
        ref[index, way, 0:half, :] = block[:, :main]
        if main < rows:
            for i in range(2):
                ref[index, way, half:, i * 64:(i + 1) * 64] = block[
                    i * half // 2:(i + 1) * half // 2, main:
                ]

    def place_block(d, way):
        main = main_lanes(rows)
        top, at = way * half, d * rows
        left[top:top + half, at:at + main] = left_in[d, way, 0:half, :]
        if main < rows:
            for i in range(2):
                left[top + i * half // 2:top + (i + 1) * half // 2, at + main:at + rows] = (
                    left_in[d, way, half:, i * 64:(i + 1) * 64]
                )

    barrier = pltpu.get_barrier_semaphore()

    def greet(i, carry):
        other = ring_row((place + i) % n, n)
        pl.semaphore_signal(barrier, inc=1, device_id=(t, other), device_id_type=MESH)
        return carry

    lax.fori_loop(1, n, greet, 0)

    @pl.when(t > 0)
    def _():
        pl.semaphore_signal(barrier, inc=1, device_id=(t - 1, r), device_id_type=MESH)

    @pl.when(t < last)
    def _():
        pl.semaphore_signal(barrier, inc=1, device_id=(t + 1, r), device_id_type=MESH)

    pl.semaphore_wait(barrier, n - 1 + (t + last - 1) // last + (2 * last - t - 1) // last)

    def cov_copy(source, j):
        columns = pl.ds(aligned(j * part, part), part)
        return pltpu.make_async_remote_copy(
            src_ref=source.at[:, columns],
            dst_ref=cov_next.at[:, columns],
            send_sem=cov_send.at[j],
            recv_sem=cov_recv.at[j],
            device_id=(t - 1, r),
            device_id_type=MESH,
        )

    def mean_copy():
        return pltpu.make_async_remote_copy(
            src_ref=mean_send,
            dst_ref=mean_next,
            send_sem=mean_sems.at[0],
            recv_sem=mean_sems.at[1],
            device_id=(t - 1, r),
            device_id_type=MESH,
        )

    def offset_copy(i):
        other = ring_row((place + i) % n, n)
        return pltpu.make_async_remote_copy(
            src_ref=offset_in,
            dst_ref=offsets.at[r],
            send_sem=offset_send.at[i],
            recv_sem=offset_recv.at[r],
            device_id=(t, other),
            device_id_type=MESH,
        )

    def offset_arrival(i):
        other = ring_row((place + i) % n, n)
        return pltpu.make_async_remote_copy(
            src_ref=offset_in,
            dst_ref=offsets.at[other],
            send_sem=offset_send.at[i],
            recv_sem=offset_recv.at[other],
            device_id=(t, other),
            device_id_type=MESH,
        )

    def ring_copy(way, hop, c):
        origin = ring_row((place + (n - hop if way == 0 else hop)) % n, n)
        span = pl.ds(aligned(origin * rows + way * half + c * piece, piece), piece)
        return pltpu.make_async_remote_copy(
            src_ref=gain.at[span, :],
            dst_ref=gain.at[span, :],
            send_sem=ring_send.at[way, hop, c],
            recv_sem=ring_recv.at[way, hop, c],
            device_id=(t, right if way == 0 else back),
            device_id_type=MESH,
        )

    def ring_arrival(way, hop, c):
        origin = ring_row((place + (n - 1 - hop if way == 0 else hop + 1)) % n, n)
        span = pl.ds(aligned(origin * rows + way * half + c * piece, piece), piece)
        return pltpu.make_async_remote_copy(
            src_ref=gain.at[span, :],
            dst_ref=gain.at[span, :],
            send_sem=ring_send.at[way, hop, c],
            recv_sem=ring_recv.at[way, hop, c],
            device_id=(t, right if way == 0 else back),
            device_id_type=MESH,
        )

    def left_copy(d, way):
        return pltpu.make_async_remote_copy(
            src_ref=left_out.at[d, way],
            dst_ref=left_in.at[r, way],
            send_sem=left_send.at[way, d],
            recv_sem=left_recv.at[way, r],
            device_id=(t, d),
            device_id_type=MESH,
        )

    def left_arrival(d, way):
        return pltpu.make_async_remote_copy(
            src_ref=left_out.at[d, way],
            dst_ref=left_in.at[d, way],
            send_sem=left_send.at[way, d],
            recv_sem=left_recv.at[way, d],
            device_id=(t, d),
            device_id_type=MESH,
        )

    def await_cov():
        for j in range(GROUPS):
            cov_copy(cov_in, j).wait_recv()

    own_cov.wait()

    @pl.when(t == last)
    def _():
        for j in range(GROUPS):
            cov_copy(cov_in, j).start()

    def send_offset(i, carry):
        offset_copy(i).start()
        return carry

    lax.fori_loop(1, n, send_offset, 0)
    own_gain.wait()

    def left_half(d, way):
        block = gain[pl.ds(aligned(d * rows + way * half, half), half), :]
        product = lax.dot_general(
            block, cov_next[...], CONTRACT_LAST, preferred_element_type=jnp.float32
        )
        return product.astype(jnp.bfloat16)

    @pl.when(t < last)
    def _():
        @pl.when(t % 2 == 0)
        def _():
            @pl.when(t < last - 1)
            def _():
                pl.semaphore_wait(gate, 1)

        for c in range(chunks):
            for way in range(2):
                ring_copy(way, 0, c).start()

        @pl.when(t == last - 1)
        def _():
            await_cov()
            for way in range(2):
                store_block(left_in, r, way, left_half(r, way))

        def pass_on(hop, carry):
            for c in range(chunks):
                for way in range(2):
                    ring_arrival(way, hop - 1, c).wait_recv()
                    ring_copy(way, hop, c).start()

            @pl.when(hop == min(HEAD_START, n - 2))
            def _():
                @pl.when(t % 2 == 1)
                def _():
                    pl.semaphore_signal(gate, inc=1, device_id=(t - 1, r), device_id_type=MESH)

            @pl.when(t == last - 1)
            def _():
                for way in range(2):
                    d = ring_row((place + (n - hop if way == 0 else hop)) % n, n)
                    store_block(left_out, d, way, left_half(d, way))
                    left_copy(d, way).start()

            return carry

        lax.fori_loop(1, n - 1, pass_on, 0)

        for c in range(chunks):
            for way in range(2):
                ring_arrival(way, n - 2, c).wait_recv()

        @pl.when(t == last - 1)
        def _():
            for way in range(2):
                d = ring_row((place + (1 if way == 0 else n - 1)) % n, n)
                store_block(left_out, d, way, left_half(d, way))
                left_copy(d, way).start()

    offsets[r] = offset_in[...]

    def await_offset(i, carry):
        offset_arrival(i).wait_recv()
        return carry

    lax.fori_loop(1, n, await_offset, 0)
    whole_offset = offsets[0]
    for i in range(1, n):
        whole_offset = whole_offset + offsets[i]

    @pl.when(t == last)
    def _():
        mean_send[...] = whole_offset
        mean_copy().start()
        mean_out[...] = whole_offset
        cov_out[...] = cov_in[...]

    @pl.when(t < last)
    def _():
        @pl.when(t < last - 1)
        def _():
            await_cov()

            def left_part(j, carry):
                g = (r // per + 1 + j) % LEFT_GROUPS
                span = pl.ds(aligned(g * left_part_rows, left_part_rows), left_part_rows)
                product = lax.dot_general(
                    gain[span, :], cov_next[...], CONTRACT_LAST,
                    preferred_element_type=jnp.float32,
                ).astype(jnp.bfloat16)
                for i in range(per):
                    d = g * per + i
                    for way in range(2):
                        top = i * rows + way * half
                        store_block(left_out, d, way, product[top:top + half])

                def send(i, carry):
                    d = g * per + (r + i) % per

                    @pl.when(d != r)
                    def _():
                        for way in range(2):
                            left_copy(d, way).start()

                    return carry

                lax.fori_loop(0, per, send, 0)
                return carry

            lax.fori_loop(0, LEFT_GROUPS, left_part, 0)
            left_in[r] = left_out[r]

        mean_copy().wait_recv()
        left[rows:, :] = jnp.broadcast_to(mean_next[...], (PAD, size)).astype(jnp.bfloat16)

        near = r // per

        def gather_half(h):
            for i in range(per):
                d = h * per + i

                @pl.when(d != r)
                def _():
                    for way in range(2):
                        left_arrival(d, way).wait_recv()

            for g in range(LEFT_GROUPS):
                @pl.when(h == g)
                def _():
                    for i in range(per):
                        for way in range(2):
                            place_block(g * per + i, way)

            return pl.ds(aligned(h * left_part_rows, left_part_rows), left_part_rows)

        near_inner = gather_half(near)

        def near_part(j, carry):
            columns = pl.ds(aligned(j * left_part_rows, left_part_rows), left_part_rows)
            partial[:, columns] = lax.dot_general(
                left[:, near_inner], gain[columns, near_inner], CONTRACT_LAST,
                preferred_element_type=jnp.float32,
            )
            return carry

        lax.fori_loop(0, LEFT_GROUPS, near_part, 0)
        far_inner = gather_half(1 - near)
        offsets[0] = whole_offset

        def right_part(j, carry):
            columns = pl.ds(aligned(j * part, part), part)
            product = partial[:, columns] + lax.dot_general(
                left[:, far_inner], gain[columns, far_inner], CONTRACT_LAST,
                preferred_element_type=jnp.float32,
            )
            cov_out[:, columns] = (
                product[:rows] + cov_in[:, columns].astype(jnp.float32)
            ).astype(jnp.bfloat16)
            mean = product[rows:rows + 1] + offsets[0, :, columns]
            mean_send[:, columns] = mean.astype(jnp.bfloat16).astype(jnp.float32)

            @pl.when(t > 0)
            def _():
                cov_copy(cov_out, j).start()

            return carry

        lax.fori_loop(0, GROUPS, right_part, 0)
        mean_out[...] = mean_send[...]

        @pl.when(t > 0)
        def _():
            mean_copy().start()

        def left_gone(i, carry):
            for way in range(2):
                left_copy(ring_row((place + i) % n, n), way).wait_send()
            return carry

        lax.fori_loop(1, n, left_gone, 0)

        def ring_gone(hop, carry):
            for c in range(chunks):
                for way in range(2):
                    ring_copy(way, hop, c).wait_send()
            return carry

        lax.fori_loop(0, n - 1, ring_gone, 0)

    @pl.when(t > 0)
    def _():
        for j in range(GROUPS):
            cov_copy(cov_out, j).wait_send()
        mean_copy().wait_send()

    def offset_gone(i, carry):
        offset_copy(i).wait_send()
        return carry

    lax.fori_loop(1, n, offset_gone, 0)


def shards(steps, n, smoother_gains, smoother_offsets, smoother_covs):
    own_gain = smoother_gains[0]
    own_cov = smoother_covs[0]
    rows, size = own_cov.shape
    start = lax.axis_index("rows") * rows
    offset_row = lax.dynamic_update_slice(
        jnp.zeros((1, size), jnp.float32), smoother_offsets.astype(jnp.float32), (0, start)
    )
    vmem = pl.BlockSpec(memory_space=pltpu.VMEM)
    hbm = pl.BlockSpec(memory_space=pltpu.HBM)
    lanes = main_lanes(rows)
    folded = (n, 2, rows // 2 * rows // lanes, lanes)
    dma = pltpu.SemaphoreType.DMA
    mean_row, cov = pl.pallas_call(
        functools.partial(kernel, steps, n),
        out_shape=(
            jax.ShapeDtypeStruct((1, size), jnp.float32),
            jax.ShapeDtypeStruct((rows, size), jnp.bfloat16),
        ),
        in_specs=[hbm, vmem, hbm],
        out_specs=(vmem, vmem),
        scratch_shapes=[
            pltpu.VMEM((size, size), jnp.bfloat16),
            pltpu.VMEM((rows, size), jnp.bfloat16),
            pltpu.VMEM((rows, size), jnp.bfloat16),
            pltpu.VMEM(folded, jnp.bfloat16),
            pltpu.VMEM(folded, jnp.bfloat16),
            pltpu.VMEM((rows + PAD, size), jnp.bfloat16),
            pltpu.VMEM((n, 1, size), jnp.float32),
            pltpu.VMEM((1, size), jnp.float32),
            pltpu.VMEM((1, size), jnp.float32),
            dma,
            dma((2, n, rows // 2 // PIECE)),
            dma((2, n, rows // 2 // PIECE)),
            dma((2, n)),
            dma((2, n)),
            dma((n,)),
            dma((n,)),
            dma((GROUPS,)),
            dma((GROUPS,)),
            dma((2,)),
            dma,
            pltpu.VMEM((rows + PAD, size), jnp.float32),
            pltpu.SemaphoreType.REGULAR,
        ],
        compiler_params=pltpu.CompilerParams(
            collective_id=0, has_side_effects=True, vmem_limit_bytes=40 << 20
        ),
    )(pltpu.with_memory_space_constraint(own_gain, pltpu.HBM), offset_row, pltpu.with_memory_space_constraint(own_cov, pltpu.HBM))
    mean = lax.dynamic_slice(mean_row, (0, start), (1, rows)).astype(jnp.bfloat16)
    return mean, cov[None]


def solution(mesh):
    in_specs = (P("tm", "rows", None), P("tm", "rows"), P("tm", "rows", None))
    out_specs = (P("tm", "rows"), P("tm", "rows", None))
    body = functools.partial(shards, mesh.shape["tm"], mesh.shape["rows"])
    return jax.shard_map(body, mesh=mesh, in_specs=in_specs, out_specs=out_specs, check_vma=False)
```
